32 devices in a mesh: parts: 2 (over y), dp: 4 (over x, core), tp: 4 (over z).
Axes of the slice: x: 2, y: 2, z: 4, core: 2. Of those that a mesh axis runs over, the one named last changes fastest.
Arguments:
- hidden: bfloat16 [32, 128, 8192], P(('parts', 'dp'), 'tp'), parts along dimension 0, may hold values from -6 to 6
- norm_gain: bfloat16 [8192], replicated, may hold values from 0.099609375 to 1.8984375
- w_query: bfloat16 [8192, 4096], P(None, 'tp'), may hold values from -0.0625 to 0.0625
- w_keyval: bfloat16 [8192, 1024], P(None, 'tp'), may hold values from -0.0625 to 0.0625
- w_out: bfloat16 [4096, 8192], P('tp'), may hold values from -0.5 to 0.5
- kv_cache: bfloat16 [1024, 16, 32, 256], P(('parts', 'dp'), 'tp'), parts along dimension 0, may hold values from -600 to 600
- page_table: int32 [32, 32], P(('parts', 'dp')), parts along dimension 0, may hold values from 0 to 127, as said below
- prefix_len: int32 [32], P(('parts', 'dp')), parts along dimension 0, may hold values from 0 to 4096, as said below
- live_rows: int32 [32], P(('parts', 'dp')), parts along dimension 0, may hold values from 1 to 128
- plan: int32 [32], P(('parts', 'dp')), parts along dimension 0, may hold values from 0 to 3, as said below
Outputs:
- result: bfloat16 [32, 128, 8192], P(('parts', 'dp'), 'tp'), parts along dimension 0
- new_kv: bfloat16 [32, 128, 1024], P(('parts', 'dp'), None, 'tp'), parts along dimension 0
The draws below stay inside these ranges and needn't reach their ends.
There are 2 independent parts, one for each index of `parts`. The reference program is written for one: setup_inputs(seed, part) draws one part's arguments, and reference() takes and returns one part's arrays. A program takes and returns all parts, laid end to end along the dimension named above; an argument that names none is the same for every part. Nothing has to cross between parts.
Inputs may be any that keep to these rules, and one draw needn't show every extreme that they name: `page_table`: the 32 pages listed for a stretch belong to its own group, and no page is listed twice within a group. `prefix_len`: a multiple of 128; within a group it never grows with the slot number. `plan`: the 4 stretches of one group go to different groups, and every group receives exactly one stretch of each slot number.
All inputs are finite; a program needn't handle non-finite values.
Results may differ from the reference program's by a relative error of at most 0.02.
The reference program's roundings to bfloat16 on the way count: a program that leaves them out, or rounds other values in their place, can miss the bound.
Values may be sent and summed in bfloat16 or wider, within the bound.
No kernel may reach another device: no remote copies, remote signals or barrier semaphores. Data moves between devices by JAX's collectives and lax.ppermute only.
A program may use at most 128 MiB of HBM per device.

```python
import math
import jax
import jax.numpy as jnp
from jax import lax

D = 8192
HEADS = 32
KV_HEADS = 4
HEAD_DIM = 128
SPLIT = 4
BLOCK = 128
MAX_PAGES = 32
OWN = 4
STRETCH = 128
GROUPS = 4
STRETCHES = 16
POOL = 128
N_TP = 4


def draw_kv_cache(key, part):
    shape = (GROUPS * POOL, KV_HEADS * SPLIT, BLOCK // SPLIT, 2 * HEAD_DIM)
    first_key = jax.random.fold_in(jax.random.fold_in(key, 71), 0)
    values = jnp.clip(jax.random.normal(first_key, shape, jnp.float32), -6.0, 6.0)
    return values.astype(jnp.bfloat16)


def draw_page_table(key, part):
    group_keys = jax.random.split(jax.random.fold_in(key, 11), GROUPS)
    orders = jax.vmap(lambda single: jax.random.permutation(single, POOL))(group_keys)
    return orders.reshape(GROUPS * OWN, MAX_PAGES).astype(jnp.int32)


def draw_prefix_len(key, part):
    first_key, second_key, third_key = jax.random.split(jax.random.fold_in(key, 23), 3)
    levels = jax.random.randint(first_key, (GROUPS, 1), 1, 5)
    raw_pages = jax.random.randint(second_key, (GROUPS, OWN), 0, MAX_PAGES + 1)
    page_counts = raw_pages * levels // 4
    heavy = jax.random.randint(third_key, (), 0, GROUPS)
    corner = (jnp.arange(GROUPS)[:, None] == heavy) & (jnp.arange(OWN)[None, :] == 0)
    page_counts = jnp.where(corner, MAX_PAGES, page_counts)
    page_counts = -jnp.sort(-page_counts, axis=1)
    return (page_counts * BLOCK).reshape(GROUPS * OWN).astype(jnp.int32)


def draw_live_rows(key, part):
    first_key, second_key, third_key = jax.random.split(jax.random.fold_in(key, 37), 3)
    whole = jax.random.randint(first_key, (STRETCHES,), 0, 2)
    shorter = jax.random.randint(second_key, (STRETCHES,), 1, STRETCH + 1)
    counts = jnp.where(whole == 1, STRETCH, shorter)
    forced = jax.random.randint(third_key, (), 0, STRETCHES)
    counts = jnp.where(jnp.arange(STRETCHES) == forced, STRETCH, counts)
    return counts.astype(jnp.int32)


def draw_plan(key, part):
    lengths = draw_prefix_len(key, part).reshape(GROUPS, OWN)
    loads = jnp.sum(lengths // BLOCK, axis=1).astype(jnp.int32)
    group_ids = jnp.arange(GROUPS, dtype=jnp.int32)
    scores = loads * GROUPS + group_ids
    order = jnp.argsort(-scores).astype(jnp.int32)
    ranking = jnp.zeros((GROUPS,), jnp.int32).at[order].set(group_ids)
    slot_ids = jnp.arange(OWN, dtype=jnp.int32)
    target_rank = (GROUPS - 1 - ranking[:, None] + slot_ids[None, :]) % GROUPS
    targets = order[target_rank]
    return targets.reshape(STRETCHES).astype(jnp.int32)


def shard_levels(key, shape, cuts, least, high):
    level = 1.0
    for position, blocks in cuts:
        heights = jax.random.uniform(jax.random.fold_in(jax.random.fold_in(key, 6), position), (blocks,), jnp.float32, least / len(cuts), high / len(cuts))
        level = level * jnp.repeat(jnp.exp(heights), shape[position] // blocks).reshape((-1,) + (1,) * (len(shape) - 1 - position))
    return level


def bell_draw(rng, extent, width, reach, cuts=(), kind=jnp.bfloat16):
    array = width * jax.random.normal(rng, extent, jnp.float32)
    if cuts:
        array = array * shard_levels(rng, extent, cuts, -0.22, 0.18)
    return jnp.clip(array, -reach, reach).astype(kind)


def setup_inputs(seed: int = 0, part: int = 0) -> dict:
    seeds = jax.random.split(jax.random.key(seed), 11)
    part_splits = jax.random.split(jax.random.fold_in(seeds[10], part), 11)
    hidden = bell_draw(part_splits[0], (STRETCHES, STRETCH, D), 1.0, 6.0, ((0, 4), (1, 4)))
    norm_gain = jnp.clip(1.0 + 0.18 * jax.random.normal(seeds[1], (D,), jnp.float32), 0.099609375, 1.8984375).astype(jnp.bfloat16)
    w_query = bell_draw(seeds[2], (D, HEADS * HEAD_DIM), D ** -0.5, 0.0625, ((1, 4),))
    w_keyval = bell_draw(seeds[3], (D, KV_HEADS * 2 * HEAD_DIM), D ** -0.5, 0.0625, ((1, 4),))
    w_out = bell_draw(seeds[4], (HEADS * HEAD_DIM, D), HEAD_DIM ** -0.5, 0.5, ((0, 4),))
    kv_cache = draw_kv_cache(jax.random.fold_in(jax.random.fold_in(seeds[10], part), 71), part)
    page_table = draw_page_table(jax.random.fold_in(jax.random.fold_in(seeds[10], part), 71), part)
    prefix_len = draw_prefix_len(jax.random.fold_in(jax.random.fold_in(seeds[10], part), 71), part)
    live_rows = draw_live_rows(jax.random.fold_in(jax.random.fold_in(seeds[10], part), 71), part)
    plan = draw_plan(jax.random.fold_in(jax.random.fold_in(seeds[10], part), 71), part)
    return dict(hidden=hidden, norm_gain=norm_gain, w_query=w_query, w_keyval=w_keyval, w_out=w_out, kv_cache=kv_cache, page_table=page_table, prefix_len=prefix_len, live_rows=live_rows, plan=plan)


EPSILON = 1e-05
ROPE_BASE = 500000.0
MASKED = -1e+30

def rotate(values, positions):
    half_width = values.shape[-1] // 2
    frequency = ROPE_BASE ** (-jnp.arange(half_width, dtype=jnp.float32) / half_width)
    angles = positions.astype(jnp.float32)[..., None] * frequency
    cosine = jnp.cos(angles)[..., None, :]
    sine_values = jnp.sin(angles)[..., None, :]
    front_half = values[..., :half_width]
    back_half = values[..., half_width:]
    return jnp.concatenate([front_half * cosine - back_half * sine_values, back_half * cosine + front_half * sine_values], axis=-1)

def one_stretch(stretch_id, hidden, norm_gain, w_query, w_keyval, out_wide, kv_cache, page_table, prefix_len, live_rows):
    stretch_rows = hidden[stretch_id]
    owner_group = stretch_id // OWN
    widened = stretch_rows.astype(jnp.float32)
    normed = (widened * lax.rsqrt(lax.optimization_barrier(jnp.mean(widened * widened, axis=-1, keepdims=True)) + EPSILON) * norm_gain.astype(jnp.float32)).astype(jnp.bfloat16)
    start_pos = prefix_len[stretch_id]
    positions = start_pos + jnp.arange(STRETCH, dtype=jnp.int32)
    queries = rotate(jnp.dot(normed, w_query, preferred_element_type=jnp.float32).reshape(STRETCH, HEADS, HEAD_DIM), positions).astype(jnp.bfloat16)
    pairs = jnp.dot(normed, w_keyval, preferred_element_type=jnp.float32).astype(jnp.bfloat16).reshape(STRETCH, KV_HEADS, 2 * HEAD_DIM)
    rotated = rotate(pairs[..., :HEAD_DIM].astype(jnp.float32), positions)
    row_index = jnp.arange(STRETCH, dtype=jnp.int32)
    live_mask = row_index < live_rows[stretch_id]
    new_pairs = (jnp.concatenate([rotated, pairs[..., HEAD_DIM:].astype(jnp.float32)], axis=-1) * live_mask[:, None, None].astype(jnp.float32)).astype(jnp.bfloat16)
    page_ids = (owner_group * POOL + page_table[stretch_id]).astype(jnp.int32)
    stored = kv_cache[page_ids].reshape(MAX_PAGES, KV_HEADS, BLOCK, 2 * HEAD_DIM)
    stored = jnp.transpose(stored, (1, 0, 2, 3)).reshape(KV_HEADS, MAX_PAGES * BLOCK, 2 * HEAD_DIM)
    every_pair = jnp.concatenate([stored, jnp.transpose(new_pairs, (1, 0, 2))], axis=1).astype(jnp.float32)
    grouped = queries.astype(jnp.float32).reshape(STRETCH, KV_HEADS, HEADS // KV_HEADS, HEAD_DIM)
    scores = jnp.einsum('cgqd,gtd->gqct', grouped, every_pair[..., :HEAD_DIM]) * (1.0 / math.sqrt(HEAD_DIM))
    key_place = jnp.arange(MAX_PAGES * BLOCK, dtype=jnp.int32)
    prefix_mask = jnp.broadcast_to(key_place[None, :] < start_pos, (STRETCH, MAX_PAGES * BLOCK))
    own_mask = (row_index[None, :] <= row_index[:, None]) & live_mask[None, :]
    full_mask = jnp.concatenate([prefix_mask, own_mask], axis=1)
    scores = jnp.where(full_mask[None, None], scores, MASKED)
    peak = lax.optimization_barrier(jnp.max(scores, axis=-1, keepdims=True))
    exps = jnp.exp(scores - peak)
    weights = (exps / lax.optimization_barrier(jnp.sum(exps, axis=-1, keepdims=True))).astype(jnp.bfloat16)
    attended = jnp.einsum('gqct,gtd->cgqd', weights.astype(jnp.float32), every_pair[..., HEAD_DIM:]).astype(jnp.bfloat16)
    group_width = HEADS * HEAD_DIM // N_TP
    attended = attended.astype(jnp.float32).reshape(STRETCH, N_TP, group_width)
    partial_value = jnp.einsum('cnk,nkd->ncd', attended, out_wide.reshape(N_TP, group_width, D)).astype(jnp.bfloat16)
    branch = lax.optimization_barrier(jnp.sum(partial_value.astype(jnp.float32), axis=0))
    branch = jnp.where(live_mask[:, None], branch, jnp.zeros_like(branch)).astype(jnp.bfloat16)
    return (branch, new_pairs.reshape(STRETCH, KV_HEADS * 2 * HEAD_DIM))

def reference(hidden, norm_gain, w_query, w_keyval, w_out, kv_cache, page_table, prefix_len, live_rows, plan):
    out_wide = w_out.astype(jnp.float32)

    def per_stretch(stretch_id):
        return one_stretch(stretch_id, hidden, norm_gain, w_query, w_keyval, out_wide, kv_cache, page_table, prefix_len, live_rows)
    branches, new_kv = lax.map(per_stretch, jnp.arange(STRETCHES, dtype=jnp.int32))
    places = (plan * OWN + jnp.arange(STRETCHES, dtype=jnp.int32) % OWN).astype(jnp.int32)
    result = jnp.zeros_like(branches).at[places].set(branches)
    return (result, new_kv)
```

```python
import functools
import math

import jax
import jax.numpy as jnp
from jax import lax
from jax.experimental import pallas as pl
from jax.experimental.pallas import tpu as pltpu
from jax.sharding import PartitionSpec as P


KV_HEADS = 4
HEAD_DIM = 128
BLOCK = 128
MAX_PAGES = 32


EPSILON = 1e-05
ROPE_BASE = 500000.0
MASKED = -1e30
HBM = pl.BlockSpec(memory_space=pltpu.MemorySpace.HBM)


def from_partner(value, axis, distance):
    mask = 2**distance
    pairs = [(source, source ^ mask) for source in range(lax.axis_size(axis))]
    return lax.ppermute(value, axis, pairs)


def rotate(values, positions):
    half_width = values.shape[-1] // 2
    frequency = ROPE_BASE ** (-jnp.arange(half_width, dtype=jnp.float32) / half_width)
    angles = positions.astype(jnp.float32)[..., None] * frequency
    cosine = jnp.cos(angles)[..., None, :]
    sine_values = jnp.sin(angles)[..., None, :]
    front_half = values[..., :half_width]
    back_half = values[..., half_width:]
    return jnp.concatenate(
        [
            front_half * cosine - back_half * sine_values,
            back_half * cosine + front_half * sine_values,
        ],
        axis=-1,
    )


def attend_one(inputs):
    queries, head_pairs, prefix, start, count = inputs
    head_width = queries.shape[-1]
    scaling = 1.0 / math.sqrt(head_width)
    row_count = queries.shape[0]
    row_index = jnp.arange(row_count, dtype=jnp.int32)
    own_mask = (row_index[None, :] <= row_index[:, None]) & (row_index[None, :] < count)
    own_scores = (
        jnp.einsum(
            "chd,jd->hcj", queries, head_pairs[:, :head_width], preferred_element_type=jnp.float32
        )
        * scaling
    )
    own_scores = jnp.where(own_mask[None], own_scores, MASKED)
    span_pages = max(1, min(MAX_PAGES, 512 // BLOCK))
    key_span = span_pages * BLOCK
    block_count = (start + key_span - 1) // key_span

    def block_scores(block_id):
        key_block = lax.dynamic_slice_in_dim(prefix, block_id * key_span, key_span, 0)
        scores = (
            jnp.einsum(
                "chd,td->hct",
                queries,
                key_block[:, :head_width],
                preferred_element_type=jnp.float32,
            )
            * scaling
        )
        key_place = block_id * key_span + jnp.arange(key_span, dtype=jnp.int32)
        key_mask = key_place < start
        return (jnp.where(key_mask[None, None, :], scores, MASKED), key_block)

    running_max = jnp.max(own_scores, axis=-1)
    running_sum = jnp.sum(jnp.exp(own_scores - running_max[..., None]), axis=-1)

    def first_pass(block_id, state_pair):
        old_max, old_sum = state_pair
        scores, key_block = block_scores(block_id)
        raised_max = jnp.maximum(old_max, jnp.max(scores, axis=-1))
        new_sum = old_sum * jnp.exp(old_max - raised_max) + jnp.sum(
            jnp.exp(scores - raised_max[..., None]), axis=-1
        )
        return (raised_max, new_sum)

    running_max, running_sum = lax.fori_loop(0, block_count, first_pass, (running_max, running_sum))

    def normalize(scores):
        return (jnp.exp(scores - running_max[..., None]) / running_sum[..., None]).astype(
            jnp.bfloat16
        )

    attended = jnp.einsum(
        "hcj,jd->chd",
        normalize(own_scores),
        head_pairs[:, head_width:],
        preferred_element_type=jnp.float32,
    )

    def second_pass(block_id, gathered_sum):
        scores, key_block = block_scores(block_id)
        return gathered_sum + jnp.einsum(
            "hct,td->chd",
            normalize(scores),
            key_block[:, head_width:],
            preferred_element_type=jnp.float32,
        )

    attended = lax.fori_loop(0, block_count, second_pass, attended)
    return attended.astype(jnp.bfloat16)


def attend(queries, head_pairs, prefix, starts, counts):
    return lax.map(attend_one, (queries, head_pairs, prefix, starts, counts))


def layer(stretch_rows, stretch_pages, starts, counts, norm_gain, w_query, w_keyval, w_out):
    tensor_size = lax.axis_size("tp")
    tensor_rank = lax.axis_index("tp")
    widened = stretch_rows.astype(jnp.float32)
    normed = (
        widened
        * lax.rsqrt(jnp.mean(widened * widened, axis=-1, keepdims=True) + EPSILON)
        * norm_gain.astype(jnp.float32)
    ).astype(jnp.bfloat16)
    query_width = w_query.shape[1]
    portion = lax.all_gather(normed, "tp", axis=1, tiled=True)
    query_part = jnp.einsum("ocd,dk->ock", portion, w_query, preferred_element_type=jnp.float32)
    pair_part = jnp.einsum("ocd,dk->ock", portion, w_keyval, preferred_element_type=jnp.float32)
    projected = jnp.concatenate([query_part, pair_part], axis=-1)
    holding = projected.shape[0]
    length = projected.shape[1]
    head_width = HEAD_DIM
    positions = starts[:, None] + jnp.arange(length, dtype=jnp.int32)[None, :]
    queries = rotate(
        projected[..., :query_width].reshape(
            holding, length, query_width // head_width, head_width
        ),
        positions,
    ).astype(jnp.bfloat16)
    pair_piece = projected[..., query_width:].astype(jnp.bfloat16)
    sharers = tensor_size // KV_HEADS
    levels = sharers.bit_length() - 1
    sharer_rank = tensor_rank % sharers
    page_piece = stretch_pages
    for level_bit in range(levels):
        their_pairs, their_pages = from_partner((pair_piece, page_piece), "tp", level_bit)
        upper_half = tensor_rank // (1 << level_bit) % 2 == 1
        pair_piece = jnp.where(
            upper_half,
            jnp.concatenate([their_pairs, pair_piece], axis=-1),
            jnp.concatenate([pair_piece, their_pairs], axis=-1),
        )
        page_piece = jnp.where(
            upper_half,
            jnp.concatenate([their_pages, page_piece], axis=2),
            jnp.concatenate([page_piece, their_pages], axis=2),
        )
    live_mask = jnp.arange(length, dtype=jnp.int32)[None, :] < counts[:, None]
    rotated_keys = rotate(
        pair_piece[..., :head_width].astype(jnp.float32)[:, :, None, :], positions
    )[:, :, 0, :]
    head_pairs = (
        jnp.concatenate([rotated_keys, pair_piece[..., head_width:].astype(jnp.float32)], axis=-1)
        * live_mask[..., None].astype(jnp.float32)
    ).astype(jnp.bfloat16)
    piece_width = 2 * head_width // sharers
    columns = lax.dynamic_slice_in_dim(head_pairs, sharer_rank * piece_width, piece_width, 2)
    prefix = page_piece.reshape(holding, -1, 2 * head_width)
    attended = attend(queries, head_pairs, prefix, starts, counts)
    partial_value = jnp.einsum(
        "ock,kd->ocd",
        attended.reshape(holding, length, -1),
        w_out,
        preferred_element_type=jnp.float32,
    )
    summed = lax.psum_scatter(
        partial_value.astype(jnp.bfloat16), "tp", scatter_dimension=1, tiled=True
    ).astype(jnp.float32)
    share_rows = summed.shape[1]
    row_ids = tensor_rank * share_rows + jnp.arange(share_rows, dtype=jnp.int32)
    keep_rows = row_ids[None, :] < counts[:, None]
    result = jnp.where(keep_rows[..., None], summed, jnp.zeros_like(summed)).astype(jnp.bfloat16)
    return (result, columns)


def general(
    hidden, norm_gain, w_query, w_keyval, w_out, kv_cache, page_table, prefix_len, live_rows, plan
):
    groups = lax.axis_size("dp")
    holding = hidden.shape[0]
    slot_ids = jnp.arange(holding, dtype=jnp.int32)
    gathered_pages = kv_cache[page_table]
    target = jnp.arange(groups, dtype=jnp.int32)
    matches = plan[None, :] == target[:, None]
    present = jnp.any(matches, axis=1)
    chosen = jnp.argmax(matches, axis=1)
    labels = jnp.where(present, chosen, -1)
    local_rows, new_kv = layer(
        hidden, gathered_pages, prefix_len, live_rows, norm_gain, w_query, w_keyval, w_out
    )
    outgoing = jnp.where(
        present[:, None, None], local_rows[chosen], jnp.zeros((), local_rows.dtype)
    )
    arrived, labels_arrived = (
        lax.all_to_all(outgoing, "dp", split_axis=0, concat_axis=0, tiled=True),
        lax.all_to_all(labels, "dp", split_axis=0, concat_axis=0, tiled=True),
    )
    source = jnp.argmax(labels_arrived[None, :] == slot_ids[:, None], axis=1)
    result = arrived[source]
    return (result, new_kv)


def norm_kernel(index_ref, hidden_ref, gain_ref, out_ref):
    widened = hidden_ref[0].astype(jnp.float32)
    mean = jnp.mean(widened * widened, axis=-1, keepdims=True)
    gain = gain_ref[...].astype(jnp.float32)
    out_ref[...] = (widened * lax.rsqrt(mean + EPSILON) * gain).astype(out_ref.dtype)


def norm_one(index, hidden, gain):
    _, rows, width = hidden.shape
    return pl.pallas_call(
        norm_kernel,
        grid_spec=pltpu.PrefetchScalarGridSpec(
            num_scalar_prefetch=1,
            grid=(1,),
            in_specs=[
                pl.BlockSpec((1, rows, width), lambda i, index_ref: (index_ref[0], 0, 0)),
                pl.BlockSpec((1, width), lambda i, index_ref: (0, 0)),
            ],
            out_specs=pl.BlockSpec((rows, width), lambda i, index_ref: (0, 0)),
        ),
        out_shape=jax.ShapeDtypeStruct((rows, width), jnp.bfloat16),
        cost_estimate=pl.CostEstimate(
            flops=4 * rows * width, bytes_accessed=4 * rows * width, transcendentals=rows
        ),
        name="norm_one",
    )(index.reshape(1), hidden, gain.reshape(1, width))


def project_kernel(sizes, head_width, depth, meta_ref, *refs):
    count = len(sizes)
    sources = refs[:count]
    query_ref, pair_ref, cosine_ref, sine_ref, turned_ref, kept_ref = refs[count : count + 6]
    rows_ref, queries_ref, pairs_ref, total, sems, query_sems, pair_sems = refs[count + 6 :]
    steps = query_sems.shape[0]
    wide = query_ref.shape[1]

    def copy(place):
        start = pl.multiple_of(meta_ref[1 + 2 * place], sizes[place])
        return pltpu.make_async_copy(
            sources[place], rows_ref.at[pl.ds(start, sizes[place])], sems.at[place]
        )

    def weight_copies(step):
        span = pl.ds(step * depth, depth)
        return (
            pltpu.make_async_copy(query_ref.at[span], queries_ref.at[step], query_sems.at[step]),
            pltpu.make_async_copy(pair_ref.at[span], pairs_ref.at[step], pair_sems.at[step]),
        )

    for place in range(count):
        @pl.when(meta_ref[2 + 2 * place] == 1)
        def _():
            copy(place).start()
    for step in range(steps):
        for item in weight_copies(step):
            item.start()
    total[...] = jnp.zeros_like(total)
    for place in range(count):
        @pl.when(meta_ref[2 + 2 * place] == 1)
        def _():
            copy(place).wait()

    @pl.loop(0, steps)
    def _(step):
        for item in weight_copies(step):
            item.wait()
        part = rows_ref[:, pl.ds(pl.multiple_of(step * depth, depth), depth)]
        total[:, :wide] += jnp.dot(part, queries_ref[step], preferred_element_type=jnp.float32)
        total[:, wide:] += jnp.dot(part, pairs_ref[step], preferred_element_type=jnp.float32)

    cosine = cosine_ref[0]
    sine = sine_ref[0]
    half = head_width // 2

    def turn(values):
        return values * cosine + pltpu.roll(values, half, 1) * sine

    for head in range(wide // head_width):
        span = slice(head * head_width, (head + 1) * head_width)
        turned_ref[:, span] = turn(total[:, span]).T.astype(turned_ref.dtype)
    keys = total[:, wide : wide + head_width].astype(jnp.bfloat16).astype(jnp.float32)
    values = total[:, wide + head_width :].astype(jnp.bfloat16).astype(jnp.float32)
    row = lax.broadcasted_iota(jnp.int32, keys.shape, 0)
    live = row < meta_ref[0]
    kept_ref[:, :head_width] = jnp.where(live, turn(keys), 0.0).astype(kept_ref.dtype)
    kept_ref[:, head_width:] = jnp.where(live, values, 0.0).astype(kept_ref.dtype)


def project(sources, places, live, index, w_query, w_keyval, cosine, sine, head_width):
    sizes = tuple(source.shape[0] for source in sources)
    width, wide = w_query.shape
    narrow = w_keyval.shape[1]
    length = cosine.shape[1]
    depth = min(width, 1024)
    steps = width // depth
    meta = [live]
    for start, used in places:
        meta += [start, used]
    meta.append(index)
    meta = jnp.stack([jnp.asarray(item, jnp.int32) for item in meta])
    last = 1 + 2 * len(sources)
    table = pl.BlockSpec((1, length, head_width), lambda k, meta_ref: (meta_ref[last], 0, 0))
    lanes = wide // head_width * length
    return pl.pallas_call(
        functools.partial(project_kernel, sizes, head_width, depth),
        grid_spec=pltpu.PrefetchScalarGridSpec(
            num_scalar_prefetch=1,
            grid=(1,),
            in_specs=[HBM] * (len(sources) + 2) + [table, table],
            out_specs=[
                pl.BlockSpec((head_width, lanes), lambda k, meta_ref: (0, 0)),
                pl.BlockSpec((length, narrow), lambda k, meta_ref: (0, 0)),
            ],
            scratch_shapes=[
                pltpu.VMEM((length, width), jnp.bfloat16),
                pltpu.VMEM((steps, depth, wide), jnp.bfloat16),
                pltpu.VMEM((steps, depth, narrow), jnp.bfloat16),
                pltpu.VMEM((length, wide + narrow), jnp.float32),
                pltpu.SemaphoreType.DMA((len(sources),)),
                pltpu.SemaphoreType.DMA((steps,)),
                pltpu.SemaphoreType.DMA((steps,)),
            ],
        ),
        out_shape=[
            jax.ShapeDtypeStruct((head_width, lanes), jnp.bfloat16),
            jax.ShapeDtypeStruct((length, narrow), jnp.bfloat16),
        ],
        compiler_params=pltpu.CompilerParams(vmem_limit_bytes=40 << 20),
        cost_estimate=pl.CostEstimate(
            flops=2 * length * width * (wide + narrow),
            bytes_accessed=2 * width * (wide + narrow) + 2 * length * width,
            transcendentals=0,
        ),
        name="project",
    )(meta, *sources, w_query, w_keyval, cosine, sine)


def stretch_kernel(sizes, length, group, tile, meta_ref, turned_ref, kept_ref, cache_ref, out_w_ref, *refs):
    count = len(sizes)
    outs = refs[:count]
    stored, weights, product, heads_ref, top_ref, sum_ref, acc_ref, page_sems, weight_sems, out_sems = refs[count:]
    block = cache_ref.shape[1]
    head_width = kept_ref.shape[1] // 2
    lanes = turned_ref.shape[1]
    pages = meta_ref[0]
    live = meta_ref[1]
    base = 2 + count
    limit = page_sems.shape[0]
    tiles = weight_sems.shape[0]
    scale = (1.0 / math.sqrt(head_width)) * math.log2(math.e)

    def page_copy(place):
        start = pl.multiple_of(place * block, block)
        return pltpu.make_async_copy(
            cache_ref.at[meta_ref[base + place]], stored.at[pl.ds(start, block)], page_sems.at[place]
        )

    def weight_copy(place):
        return pltpu.make_async_copy(
            out_w_ref.at[:, pl.ds(place * tile, tile)], weights.at[place], weight_sems.at[place]
        )

    @pl.loop(0, pages)
    def _(place):
        page_copy(place).start()

    for place in range(tiles):
        weight_copy(place).start()

    def fold(keys, values, mask):
        scores = jnp.dot(keys, turned_ref[...], preferred_element_type=jnp.float32)
        if mask is not None:
            scores = jnp.where(mask, scores, MASKED)
            top = jnp.max(scores, axis=0, keepdims=True)
        else:
            top = jnp.maximum(top_ref[...], jnp.max(scores, axis=0, keepdims=True))
        exps = jnp.exp2((scores - top) * scale)
        added = jnp.sum(exps, axis=0, keepdims=True)
        taken = lax.dot_general(
            values, exps.astype(jnp.bfloat16), (((0,), (0,)), ((), ())), preferred_element_type=jnp.float32
        )
        if mask is not None:
            sum_ref[...] = added
            acc_ref[...] = taken
        else:
            fade = jnp.exp2((top_ref[...] - top) * scale)
            sum_ref[...] = sum_ref[...] * fade + added
            acc_ref[...] = acc_ref[...] * fade + taken
        top_ref[...] = top

    key_row = lax.broadcasted_iota(jnp.int32, (length, lanes), 0)
    query_row = lax.rem(lax.broadcasted_iota(jnp.int32, (length, lanes), 1), length)
    fold(kept_ref[:, :head_width], kept_ref[:, head_width:], (key_row <= query_row) & (key_row < live))

    def fold_span(first, span):
        for item in range(span):
            page_copy(first + item).wait()
        rows = pl.ds(pl.multiple_of(first * block, block), span * block)
        fold(stored[rows, :head_width], stored[rows, head_width:], None)

    whole = pages // group

    @pl.loop(0, whole)
    def _(step):
        fold_span(step * group, group)

    @pl.loop(whole * group, pages)
    def _(place):
        fold_span(place, 1)

    share = acc_ref[...] / sum_ref[...]
    for head in range(lanes // length):
        span = slice(head * length, (head + 1) * length)
        heads_ref[:, head * head_width : (head + 1) * head_width] = share[:, span].T.astype(heads_ref.dtype)

    def out_copies(place):
        copies = []
        for item in range(count):
            start = pl.multiple_of(meta_ref[2 + item], sizes[item])
            copies.append(
                pltpu.make_async_copy(
                    product.at[place, pl.ds(start, sizes[item])],
                    outs[item].at[:, pl.ds(place * tile, tile)],
                    out_sems.at[item, place],
                )
            )
        return copies

    for place in range(tiles):
        weight_copy(place).wait()
        product[place] = jnp.dot(
            heads_ref[...], weights[place], preferred_element_type=jnp.float32
        ).astype(product.dtype)
        for item in out_copies(place):
            item.start()
    for place in range(tiles):
        for item in out_copies(place):
            item.wait()


def attend_stretch(turned, kept, cache, pages, prefix, live, w_out, spans, length):
    sizes = tuple(size for size, _ in spans)
    head_width = turned.shape[0]
    lanes = turned.shape[1]
    block = cache.shape[1]
    limit = pages.shape[0]
    inner, width = w_out.shape
    tile = min(width, 1024)
    tiles = width // tile
    meta = jnp.concatenate(
        [
            jnp.stack(
                [jnp.asarray(item, jnp.int32) for item in (prefix // block, live, *(start for _, start in spans))]
            ),
            pages,
        ]
    )
    group = min(4, limit)
    return pl.pallas_call(
        functools.partial(stretch_kernel, sizes, length, group, tile),
        grid_spec=pltpu.PrefetchScalarGridSpec(
            num_scalar_prefetch=1,
            grid=(1,),
            in_specs=[
                pl.BlockSpec(turned.shape, lambda i, meta_ref: (0, 0)),
                pl.BlockSpec(kept.shape, lambda i, meta_ref: (0, 0)),
                HBM,
                HBM,
            ],
            out_specs=[HBM] * len(sizes),
            scratch_shapes=[
                pltpu.VMEM((limit * block, 2 * head_width), jnp.bfloat16),
                pltpu.VMEM((tiles, inner, tile), jnp.bfloat16),
                pltpu.VMEM((tiles, length, tile), jnp.bfloat16),
                pltpu.VMEM((length, inner), jnp.bfloat16),
                pltpu.VMEM((1, lanes), jnp.float32),
                pltpu.VMEM((1, lanes), jnp.float32),
                pltpu.VMEM((head_width, lanes), jnp.float32),
                pltpu.SemaphoreType.DMA((limit,)),
                pltpu.SemaphoreType.DMA((tiles,)),
                pltpu.SemaphoreType.DMA((len(sizes), tiles)),
            ],
        ),
        out_shape=[jax.ShapeDtypeStruct((size, width), jnp.bfloat16) for size in sizes],
        compiler_params=pltpu.CompilerParams(vmem_limit_bytes=48 << 20),
        cost_estimate=pl.CostEstimate(
            flops=4 * lanes * head_width * limit * block + 2 * length * inner * width,
            bytes_accessed=2 * inner * width + 4 * limit * block * head_width,
            transcendentals=lanes * limit * block,
        ),
        name="attend",
    )(meta, turned, kept, cache, w_out)


def exchange(value, axis, distance):
    pairs = [(source, source ^ distance) for source in range(lax.axis_size(axis))]
    return lax.ppermute(value, axis, pairs)


def position_tables(starts, length):
    half = HEAD_DIM // 2
    frequency = ROPE_BASE ** (-jnp.arange(half, dtype=jnp.float32) / half)
    positions = starts[:, None] + jnp.arange(length, dtype=jnp.int32)[None, :]
    angles = positions.astype(jnp.float32)[..., None] * frequency
    cosine = jnp.cos(angles)
    sine = jnp.sin(angles)
    return (
        jnp.concatenate([cosine, cosine], axis=-1),
        jnp.concatenate([-sine, sine], axis=-1),
    )


def added(*terms):
    return functools.reduce(lambda a, b: a + b, [term.astype(jnp.float32) for term in terms])


def paired(
    hidden, norm_gain, w_query, w_keyval, w_out, kv_cache, page_table, prefix_len, live_rows, plan
):
    groups = lax.axis_size("dp")
    group = lax.axis_index("dp")
    rank = lax.axis_index("tp")
    holding, share, width = hidden.shape
    length = share * lax.axis_size("tp")
    upper = rank // 2
    odd = rank % 2
    inner = ((rank == 1) | (rank == 2)).astype(jnp.int32)
    cache = kv_cache.reshape(kv_cache.shape[0], -1, kv_cache.shape[-1])
    slot_ids = jnp.arange(holding, dtype=jnp.int32)
    matches = plan[None, :] == jnp.arange(groups, dtype=jnp.int32)[:, None]
    chosen = jnp.sum(jnp.where(matches, slot_ids[None, :], 0), axis=1)
    cosine, sine = position_tables(prefix_len, length)
    turns = list(range(groups))[::-1]
    picks = [chosen[group ^ turn] for turn in turns]

    normed = [norm_one(pick, hidden, norm_gain) for pick in picks]
    labels = lax.all_to_all(chosen, "dp", split_axis=0, concat_axis=0, tiled=True)

    result = jnp.zeros_like(hidden)
    kept_parts = []
    middle = [(1, 2), (2, 1)]
    outward = [(1, 0), (2, 3)]
    inward = [(0, 1), (3, 2)]
    for step, (turn, pick) in enumerate(zip(turns, picks)):
        own = normed[step]
        if step == 0:
            sources = [own] + [exchange(own, "tp", distance) for distance in (1, 2, 3)]
            places = [((rank ^ distance) * share, 1) for distance in range(4)]
        else:
            sibling = exchange(own, "tp", 1)
            pair = jnp.where(
                odd == 1,
                jnp.concatenate([sibling, own], axis=0),
                jnp.concatenate([own, sibling], axis=0),
            )
            crossed = lax.ppermute(pair, "tp", middle)
            passed = lax.ppermute(crossed, "tp", outward)
            sources = [pair, crossed, passed]
            near, far = upper * 2 * share, (1 - upper) * 2 * share
            places = [(near, 1), (far, inner), (far, 1 - inner)]
        live = live_rows[pick]
        turned, kept = project(
            sources, places, live, pick, w_query, w_keyval, cosine, sine, HEAD_DIM
        )
        kept_parts.append(kept)
        last = step == len(turns) - 1
        if last:
            spans = [(share, (rank ^ distance) * share) for distance in range(4)]
        else:
            spans = [
                (2 * share, (1 - upper) * 2 * share),
                (share, (rank ^ 1) * share),
                (share, rank * share),
            ]
        parts = attend_stretch(
            turned, kept, cache, page_table[pick], prefix_len[pick], live, w_out, spans, length
        )
        if last:
            terms = [parts[0]] + [exchange(parts[d], "tp", d) for d in (1, 2, 3)]
        else:
            far_part, sibling_part, own_part = parts
            joined = lax.ppermute(far_part, "tp", inward)
            outgoing = added(far_part, joined).astype(jnp.bfloat16)
            crossed = lax.ppermute(outgoing, "tp", middle)
            block = lambda which: lax.dynamic_slice_in_dim(crossed, which * share, share, 0)
            outgoing = added(sibling_part, block(1 - odd)).astype(jnp.bfloat16)
            terms = [own_part, block(odd), exchange(outgoing, "tp", 1)]
        row_ids = rank * share + jnp.arange(share, dtype=jnp.int32)
        branch = jnp.where((row_ids < live)[:, None], added(*terms), 0.0).astype(jnp.bfloat16)
        if turn:
            branch = exchange(branch, "dp", turn)
        result = lax.dynamic_update_slice(result, branch[None], (labels[group ^ turn], 0, 0))
    kept_all = jnp.stack(kept_parts)
    order = jnp.sum(
        jnp.where(jnp.stack(picks)[None, :] == slot_ids[:, None], slot_ids[None, :], 0), axis=1
    )
    return (result, kept_all[order])


def per_device(
    hidden, norm_gain, w_query, w_keyval, w_out, kv_cache, page_table, prefix_len, live_rows, plan
):
    groups = lax.axis_size("dp")
    ranks = lax.axis_size("tp")
    even = groups == hidden.shape[0] and groups & (groups - 1) == 0
    route = paired if even and ranks == KV_HEADS == 4 else general
    return route(
        hidden, norm_gain, w_query, w_keyval, w_out, kv_cache, page_table, prefix_len, live_rows, plan
    )


def solution(mesh):
    in_specs = (
        P(("parts", "dp"), "tp", None),
        P(),
        P(None, "tp"),
        P(None, "tp"),
        P("tp", None),
        P(("parts", "dp"), "tp", None, None),
        P(("parts", "dp"), None),
        P(("parts", "dp")),
        P(("parts", "dp")),
        P(("parts", "dp")),
    )
    out_specs = (P(("parts", "dp"), "tp", None), P(("parts", "dp"), None, "tp"))
    return jax.shard_map(
        per_device, mesh=mesh, in_specs=in_specs, out_specs=out_specs, check_vma=False
    )
```

```python
import functools
import math

import jax
import jax.numpy as jnp
from jax import lax
from jax.experimental import pallas as pl
from jax.experimental.pallas import tpu as pltpu
from jax.sharding import PartitionSpec as P


KV_HEADS = 4
HEAD_DIM = 128
BLOCK = 128
MAX_PAGES = 32


EPSILON = 1e-05
ROPE_BASE = 500000.0
MASKED = -1e30
HBM = pl.BlockSpec(memory_space=pl.ANY)
GRANT = 20 << 20


def from_partner(value, axis, distance):
    mask = 2**distance
    pairs = [(source, source ^ mask) for source in range(lax.axis_size(axis))]
    return lax.ppermute(value, axis, pairs)


def rotate(values, positions):
    half_width = values.shape[-1] // 2
    frequency = ROPE_BASE ** (-jnp.arange(half_width, dtype=jnp.float32) / half_width)
    angles = positions.astype(jnp.float32)[..., None] * frequency
    cosine = jnp.cos(angles)[..., None, :]
    sine_values = jnp.sin(angles)[..., None, :]
    front_half = values[..., :half_width]
    back_half = values[..., half_width:]
    return jnp.concatenate(
        [
            front_half * cosine - back_half * sine_values,
            back_half * cosine + front_half * sine_values,
        ],
        axis=-1,
    )


def attend_one(inputs):
    queries, head_pairs, prefix, start, count = inputs
    head_width = queries.shape[-1]
    scaling = 1.0 / math.sqrt(head_width)
    row_count = queries.shape[0]
    row_index = jnp.arange(row_count, dtype=jnp.int32)
    own_mask = (row_index[None, :] <= row_index[:, None]) & (row_index[None, :] < count)
    own_scores = (
        jnp.einsum(
            "chd,jd->hcj", queries, head_pairs[:, :head_width], preferred_element_type=jnp.float32
        )
        * scaling
    )
    own_scores = jnp.where(own_mask[None], own_scores, MASKED)
    span_pages = max(1, min(MAX_PAGES, 512 // BLOCK))
    key_span = span_pages * BLOCK
    block_count = (start + key_span - 1) // key_span

    def block_scores(block_id):
        key_block = lax.dynamic_slice_in_dim(prefix, block_id * key_span, key_span, 0)
        scores = (
            jnp.einsum(
                "chd,td->hct",
                queries,
                key_block[:, :head_width],
                preferred_element_type=jnp.float32,
            )
            * scaling
        )
        key_place = block_id * key_span + jnp.arange(key_span, dtype=jnp.int32)
        key_mask = key_place < start
        return (jnp.where(key_mask[None, None, :], scores, MASKED), key_block)

    running_max = jnp.max(own_scores, axis=-1)
    running_sum = jnp.sum(jnp.exp(own_scores - running_max[..., None]), axis=-1)

    def first_pass(block_id, state_pair):
        old_max, old_sum = state_pair
        scores, _ = block_scores(block_id)
        raised_max = jnp.maximum(old_max, jnp.max(scores, axis=-1))
        new_sum = old_sum * jnp.exp(old_max - raised_max) + jnp.sum(
            jnp.exp(scores - raised_max[..., None]), axis=-1
        )
        return (raised_max, new_sum)

    running_max, running_sum = lax.fori_loop(0, block_count, first_pass, (running_max, running_sum))

    def normalize(scores):
        return (jnp.exp(scores - running_max[..., None]) / running_sum[..., None]).astype(
            jnp.bfloat16
        )

    attended = jnp.einsum(
        "hcj,jd->chd",
        normalize(own_scores),
        head_pairs[:, head_width:],
        preferred_element_type=jnp.float32,
    )

    def second_pass(block_id, gathered_sum):
        scores, key_block = block_scores(block_id)
        return gathered_sum + jnp.einsum(
            "hct,td->chd",
            normalize(scores),
            key_block[:, head_width:],
            preferred_element_type=jnp.float32,
        )

    attended = lax.fori_loop(0, block_count, second_pass, attended)
    return attended.astype(jnp.bfloat16)


def attend(queries, head_pairs, prefix, starts, counts):
    return lax.map(attend_one, (queries, head_pairs, prefix, starts, counts))


def layer(stretch_rows, stretch_pages, starts, counts, norm_gain, w_query, w_keyval, w_out):
    tensor_size = lax.axis_size("tp")
    tensor_rank = lax.axis_index("tp")
    widened = stretch_rows.astype(jnp.float32)
    normed = (
        widened
        * lax.rsqrt(jnp.mean(widened * widened, axis=-1, keepdims=True) + EPSILON)
        * norm_gain.astype(jnp.float32)
    ).astype(jnp.bfloat16)
    query_width = w_query.shape[1]
    portion = lax.all_gather(normed, "tp", axis=1, tiled=True)
    query_part = jnp.einsum("ocd,dk->ock", portion, w_query, preferred_element_type=jnp.float32)
    pair_part = jnp.einsum("ocd,dk->ock", portion, w_keyval, preferred_element_type=jnp.float32)
    projected = jnp.concatenate([query_part, pair_part], axis=-1)
    holding = projected.shape[0]
    length = projected.shape[1]
    head_width = HEAD_DIM
    positions = starts[:, None] + jnp.arange(length, dtype=jnp.int32)[None, :]
    queries = rotate(
        projected[..., :query_width].reshape(
            holding, length, query_width // head_width, head_width
        ),
        positions,
    ).astype(jnp.bfloat16)
    pair_piece = projected[..., query_width:].astype(jnp.bfloat16)
    sharers = tensor_size // KV_HEADS
    levels = sharers.bit_length() - 1
    sharer_rank = tensor_rank % sharers
    page_piece = stretch_pages
    for level_bit in range(levels):
        their_pairs, their_pages = from_partner((pair_piece, page_piece), "tp", level_bit)
        upper_half = tensor_rank // (1 << level_bit) % 2 == 1
        pair_piece = jnp.where(
            upper_half,
            jnp.concatenate([their_pairs, pair_piece], axis=-1),
            jnp.concatenate([pair_piece, their_pairs], axis=-1),
        )
        page_piece = jnp.where(
            upper_half,
            jnp.concatenate([their_pages, page_piece], axis=2),
            jnp.concatenate([page_piece, their_pages], axis=2),
        )
    live_mask = jnp.arange(length, dtype=jnp.int32)[None, :] < counts[:, None]
    rotated_keys = rotate(
        pair_piece[..., :head_width].astype(jnp.float32)[:, :, None, :], positions
    )[:, :, 0, :]
    head_pairs = (
        jnp.concatenate([rotated_keys, pair_piece[..., head_width:].astype(jnp.float32)], axis=-1)
        * live_mask[..., None].astype(jnp.float32)
    ).astype(jnp.bfloat16)
    piece_width = 2 * head_width // sharers
    columns = lax.dynamic_slice_in_dim(head_pairs, sharer_rank * piece_width, piece_width, 2)
    prefix = page_piece.reshape(holding, -1, 2 * head_width)
    attended = attend(queries, head_pairs, prefix, starts, counts)
    partial_value = jnp.einsum(
        "ock,kd->ocd",
        attended.reshape(holding, length, -1),
        w_out,
        preferred_element_type=jnp.float32,
    )
    summed = lax.psum_scatter(
        partial_value.astype(jnp.bfloat16), "tp", scatter_dimension=1, tiled=True
    ).astype(jnp.float32)
    share_rows = summed.shape[1]
    row_ids = tensor_rank * share_rows + jnp.arange(share_rows, dtype=jnp.int32)
    keep_rows = row_ids[None, :] < counts[:, None]
    result = jnp.where(keep_rows[..., None], summed, jnp.zeros_like(summed)).astype(jnp.bfloat16)
    return (result, columns)


def general(
    hidden, norm_gain, w_query, w_keyval, w_out, kv_cache, page_table, prefix_len, live_rows, plan
):
    groups = lax.axis_size("dp")
    holding = hidden.shape[0]
    slot_ids = jnp.arange(holding, dtype=jnp.int32)
    gathered_pages = kv_cache[page_table]
    target = jnp.arange(groups, dtype=jnp.int32)
    matches = plan[None, :] == target[:, None]
    present = jnp.any(matches, axis=1)
    chosen = jnp.argmax(matches, axis=1)
    labels = jnp.where(present, chosen, -1)
    local_rows, new_kv = layer(
        hidden, gathered_pages, prefix_len, live_rows, norm_gain, w_query, w_keyval, w_out
    )
    outgoing = jnp.where(
        present[:, None, None], local_rows[chosen], jnp.zeros((), local_rows.dtype)
    )
    arrived, labels_arrived = (
        lax.all_to_all(outgoing, "dp", split_axis=0, concat_axis=0, tiled=True),
        lax.all_to_all(labels, "dp", split_axis=0, concat_axis=0, tiled=True),
    )
    source = jnp.argmax(labels_arrived[None, :] == slot_ids[:, None], axis=1)
    result = arrived[source]
    return (result, new_kv)


LINE = 4


def pick_of(info_ref, turn, holding):
    target = info_ref[1] ^ turn
    pick = 0
    for place in range(1, holding):
        pick = jnp.where(info_ref[2 + place] == target, place, pick)
    return pick


def norm_kernel(info_ref, hidden_ref, gain_ref, *out_refs):
    step = pl.program_id(0)
    widened = hidden_ref[0].astype(jnp.float32)
    mean = jnp.mean(widened * widened, axis=-1, keepdims=True)
    gain = gain_ref[...].astype(jnp.float32)[None, :]
    normed = (widened * lax.rsqrt(mean + EPSILON) * gain).astype(jnp.bfloat16)
    for place, out_ref in enumerate(out_refs):
        @pl.when(step == place)
        def _():
            out_ref[...] = normed


def norm_some(info, turns, hidden, gain):
    holding, rows, width = hidden.shape

    def chosen(i, info_ref):
        turn = jnp.int32(turns[0])
        for place in range(1, len(turns)):
            turn = jnp.where(i == place, turns[place], turn)
        return (pick_of(info_ref, turn, holding), 0, 0)

    return pl.pallas_call(
        norm_kernel,
        grid_spec=pltpu.PrefetchScalarGridSpec(
            num_scalar_prefetch=1,
            grid=(len(turns),),
            in_specs=[
                pl.BlockSpec((1, rows, width), chosen),
                pl.BlockSpec((width,), lambda i, info_ref: (0,)),
            ],
            out_specs=[pl.BlockSpec((rows, width), lambda i, info_ref: (0, 0))] * len(turns),
        ),
        out_shape=[jax.ShapeDtypeStruct((rows, width), jnp.bfloat16)] * len(turns),
        compiler_params=pltpu.CompilerParams(vmem_limit_bytes=GRANT),
        cost_estimate=pl.CostEstimate(
            flops=4 * rows * width * len(turns),
            bytes_accessed=4 * rows * width * len(turns),
            transcendentals=rows,
        ),
        name="norm_some",
    )(info, hidden, gain)


def load_kernel(count, *refs):
    sources, kept, sems = refs[:count], refs[-1 - count : -1], refs[-1]
    copies = [
        pltpu.make_async_copy(sources[place], kept[place], sems.at[place]) for place in range(count)
    ]
    for item in copies:
        item.start()
    for item in copies:
        item.wait()


def load(*arrays, after=()):
    kept = pl.BlockSpec(memory_space=pltpu.MemorySpace.VMEM)
    return pl.pallas_call(
        functools.partial(load_kernel, len(arrays)),
        in_specs=[HBM] * (len(arrays) + len(after)),
        out_specs=[kept] * len(arrays),
        out_shape=[pltpu.VMEM(item.shape, item.dtype) for item in arrays],
        scratch_shapes=[pltpu.SemaphoreType.DMA((len(arrays),))],
        compiler_params=pltpu.CompilerParams(vmem_limit_bytes=GRANT),
        name="load",
    )(*stored_of(*arrays), *after)


def stored_of(*arrays):
    return [pltpu.with_memory_space_constraint(item, pltpu.MemorySpace.HBM) for item in arrays]


def resident_of(*arrays):
    return [pltpu.with_memory_space_constraint(item, pltpu.MemorySpace.VMEM) for item in arrays]


def project_kernel(count, share, places, turn, holding, head_width, tile, aliased, info_ref, *refs):
    sources = refs[:count]
    query_ref, pair_ref, cosine_ref, sine_ref = refs[count : count + 4]
    refs = refs[count + 4 + aliased :]
    turned_ref, kept_ref, placed_ref = refs[:3]
    rows_ref, sems = refs[3:]
    wide = query_ref.shape[1]
    rank = info_ref[0]
    live = info_ref[2 + 2 * holding + pick_of(info_ref, turn, holding)]

    def copy(place):
        source, half = places[place][:2]
        start = pl.multiple_of(places[place][2](rank), share)
        return pltpu.make_async_copy(
            sources[source].at[pl.ds(half * share, share)],
            rows_ref.at[pl.ds(start, share)],
            sems.at[place],
        )

    for place in range(len(places)):
        @pl.when(places[place][3](rank))
        def _():
            copy(place).start()
    for place in range(len(places)):
        @pl.when(places[place][3](rank))
        def _():
            copy(place).wait()

    length = rows_ref.shape[0]
    cosine = cosine_ref[0]
    sine = sine_ref[0]
    half = head_width // 2

    def turn_rows(values):
        return values * cosine + pltpu.roll(values, half, 1) * sine

    @pl.loop(0, wide // tile)
    def _(step):
        span = pl.ds(pl.multiple_of(step * tile, tile), tile)
        part = jnp.dot(rows_ref[...], query_ref[:, span], preferred_element_type=jnp.float32)
        for head in range(tile // head_width):
            turned = turn_rows(part[:, head * head_width : (head + 1) * head_width])
            place = pl.ds(pl.multiple_of((step * (tile // head_width) + head) * length, length), length)
            turned_ref[:, place] = turned.T.astype(turned_ref.dtype)

    pairs = jnp.dot(rows_ref[...], pair_ref[...], preferred_element_type=jnp.float32)
    pairs = pairs.astype(jnp.bfloat16).astype(jnp.float32)
    keys, values = pairs[:, :head_width], pairs[:, head_width:]
    row = lax.broadcasted_iota(jnp.int32, keys.shape, 0)
    keys = jnp.where(row < live, turn_rows(keys), 0.0).astype(kept_ref.dtype)
    values = jnp.where(row < live, values, 0.0).astype(kept_ref.dtype)
    for target in (kept_ref, placed_ref.at[0]):
        target[:, :head_width] = keys
        target[:, head_width:] = values


def project(info, turn, sources, places, w_query, w_keyval, cosine, sine, placed):
    share = sources[0].shape[0]
    width, wide = w_query.shape
    narrow = w_keyval.shape[1]
    holding, length, head_width = cosine.shape
    tile = min(wide, 2 * head_width)
    resident = pl.BlockSpec(memory_space=pltpu.MemorySpace.VMEM)
    picked = lambda i, info_ref: (pick_of(info_ref, turn, holding), 0, 0)
    fixed = lambda i, info_ref: (0, 0)
    lanes = wide // head_width * length
    extra = [] if placed is None else [placed]
    return pl.pallas_call(
        functools.partial(
            project_kernel, len(sources), share, places, turn, holding, head_width, tile, len(extra)
        ),
        grid_spec=pltpu.PrefetchScalarGridSpec(
            num_scalar_prefetch=1,
            grid=(1,),
            in_specs=[HBM] * len(sources)
            + [resident] * 2
            + [pl.BlockSpec((1, length, head_width), picked)] * 2
            + [HBM] * len(extra),
            out_specs=[
                pl.BlockSpec((head_width, lanes), fixed),
                pl.BlockSpec((length, narrow), fixed),
                pl.BlockSpec((1, length, narrow), picked),
            ],
            scratch_shapes=[
                pltpu.VMEM((length, width), jnp.bfloat16),
                pltpu.SemaphoreType.DMA((len(places),)),
            ],
        ),
        out_shape=[
            jax.ShapeDtypeStruct((head_width, lanes), jnp.bfloat16),
            jax.ShapeDtypeStruct((length, narrow), jnp.bfloat16),
            jax.ShapeDtypeStruct((holding, length, narrow), jnp.bfloat16),
        ],
        input_output_aliases={len(sources) + 5: 2} if extra else {},
        compiler_params=pltpu.CompilerParams(vmem_limit_bytes=GRANT),
        cost_estimate=pl.CostEstimate(
            flops=2 * length * width * (wide + narrow),
            bytes_accessed=2 * length * width,
            transcendentals=0,
        ),
        name="project",
    )(info, *stored_of(*sources), *resident_of(w_query, w_keyval), cosine, sine, *extra)


def stretch_kernel(
    count, part, pieces, turn, holding, limit, length, group, tile, info_ref, turned_ref, kept_ref, cache_ref, out_w_ref, *refs
):
    outs = refs[:count]
    stored, product, heads_ref, top_ref, sum_ref, acc_ref, page_sems, out_sems = refs[count:]
    block = cache_ref.shape[1]
    head_width = kept_ref.shape[1] // 2
    lanes = turned_ref.shape[1]
    rank = info_ref[0]
    pick = pick_of(info_ref, turn, holding)
    pages = info_ref[2 + holding + pick] // block
    live = info_ref[2 + 2 * holding + pick]
    base = 2 + 3 * holding + pick * limit
    tiles = product.shape[0]
    scale = (1.0 / math.sqrt(head_width)) * math.log2(math.e)

    def page_copy(place):
        start = pl.multiple_of(place * block, block)
        return pltpu.make_async_copy(
            cache_ref.at[info_ref[base + place]], stored.at[pl.ds(start, block)], page_sems.at[place]
        )

    @pl.loop(0, pages)
    def _(place):
        page_copy(place).start()

    def fold(keys, values, mask):
        scores = jnp.dot(keys, turned_ref[...], preferred_element_type=jnp.float32)
        if mask is not None:
            scores = jnp.where(mask, scores, MASKED)
            top = jnp.max(scores, axis=0, keepdims=True)
        else:
            top = jnp.maximum(top_ref[...], jnp.max(scores, axis=0, keepdims=True))
        exps = jnp.exp2((scores - top) * scale)
        summed = jnp.sum(exps, axis=0, keepdims=True)
        taken = lax.dot_general(
            values, exps.astype(jnp.bfloat16), (((0,), (0,)), ((), ())), preferred_element_type=jnp.float32
        )
        if mask is not None:
            sum_ref[...] = summed
            acc_ref[...] = taken
        else:
            fade = jnp.exp2((top_ref[...] - top) * scale)
            sum_ref[...] = sum_ref[...] * fade + summed
            acc_ref[...] = acc_ref[...] * fade + taken
        top_ref[...] = top

    key_row = lax.broadcasted_iota(jnp.int32, (length, lanes), 0)
    query_row = lax.rem(lax.broadcasted_iota(jnp.int32, (length, lanes), 1), length)
    fold(kept_ref[:, :head_width], kept_ref[:, head_width:], (key_row <= query_row) & (key_row < live))

    def fold_span(first, span):
        for item in range(span):
            page_copy(first + item).wait()
        rows = pl.ds(pl.multiple_of(first * block, block), span * block)
        fold(stored[rows, :head_width], stored[rows, head_width:], None)

    whole = pages // group

    @pl.loop(0, whole)
    def _(step):
        fold_span(step * group, group)

    @pl.loop(whole * group, pages)
    def _(place):
        fold_span(place, 1)

    share = acc_ref[...] / sum_ref[...]
    row = lax.broadcasted_iota(jnp.int32, (length, head_width), 0)
    for head in range(lanes // length):
        span = slice(head * length, (head + 1) * length)
        heads_ref[:, head * head_width : (head + 1) * head_width] = jnp.where(
            row < live, share[:, span].T, 0.0
        ).astype(heads_ref.dtype)

    def out_copies(place):
        copies = []
        for item, (out, half, row_start) in enumerate(pieces):
            start = pl.multiple_of(row_start(rank), part)
            columns = pl.ds(pl.multiple_of(place * tile, tile), tile)
            copies.append(
                pltpu.make_async_copy(
                    product.at[place, pl.ds(start, part)],
                    outs[out].at[pl.ds(half * part, part), columns],
                    out_sems.at[item, place],
                )
            )
        return copies

    @pl.loop(0, tiles)
    def _(place):
        columns = pl.ds(pl.multiple_of(place * tile, tile), tile)
        product[place] = jnp.dot(
            heads_ref[...], out_w_ref[:, columns], preferred_element_type=jnp.float32
        ).astype(product.dtype)
        for item in out_copies(place):
            item.start()

    @pl.loop(0, tiles)
    def _(place):
        for item in out_copies(place):
            item.wait()


def attend_stretch(info, turn, turned, kept, cache, w_out, sizes, pieces, part, holding, limit, length):
    head_width, lanes = turned.shape
    block = cache.shape[1]
    inner, width = w_out.shape
    tile = min(width, 1024)
    tiles = width // tile
    group = min(4, limit)
    return pl.pallas_call(
        functools.partial(
            stretch_kernel, len(sizes), part, pieces, turn, holding, limit, length, group, tile
        ),
        grid_spec=pltpu.PrefetchScalarGridSpec(
            num_scalar_prefetch=1,
            grid=(1,),
            in_specs=[
                pl.BlockSpec(turned.shape, lambda i, info_ref: (0, 0)),
                pl.BlockSpec(kept.shape, lambda i, info_ref: (0, 0)),
                HBM,
                pl.BlockSpec(memory_space=pltpu.MemorySpace.VMEM),
            ],
            out_specs=[HBM] * len(sizes),
            scratch_shapes=[
                pltpu.VMEM((limit * block, 2 * head_width), jnp.bfloat16),
                pltpu.VMEM((tiles, length, tile), jnp.bfloat16),
                pltpu.VMEM((length, inner), jnp.bfloat16),
                pltpu.VMEM((1, lanes), jnp.float32),
                pltpu.VMEM((1, lanes), jnp.float32),
                pltpu.VMEM((head_width, lanes), jnp.float32),
                pltpu.SemaphoreType.DMA((limit,)),
                pltpu.SemaphoreType.DMA((len(pieces), tiles)),
            ],
        ),
        out_shape=[jax.ShapeDtypeStruct((size, width), jnp.bfloat16) for size in sizes],
        compiler_params=pltpu.CompilerParams(vmem_limit_bytes=GRANT),
        cost_estimate=pl.CostEstimate(
            flops=4 * lanes * head_width * limit * block + 2 * length * inner * width,
            bytes_accessed=4 * limit * block * head_width,
            transcendentals=lanes * limit * block,
        ),
        name="attend",
    )(info, turned, kept, *stored_of(cache), *resident_of(w_out))


def finish_kernel(turns, info_ref, labels_ref, *refs):
    count = len(turns) - 1
    moved_refs, terms = refs[:count], refs[count:-4]
    out_ref, last_ref, sems, last_sem = refs[-4:]
    group = info_ref[1]

    def copy(place):
        return pltpu.make_async_copy(
            moved_refs[place], out_ref.at[labels_ref[group ^ turns[place]]], sems.at[place]
        )

    for place in range(count):
        copy(place).start()
    total = terms[0][...].astype(jnp.float32)
    for term in terms[1:]:
        total += term[...].astype(jnp.float32)
    last_ref[...] = total.astype(last_ref.dtype)
    last = pltpu.make_async_copy(last_ref, out_ref.at[labels_ref[group ^ turns[count]]], last_sem)
    last.start()
    for place in range(count):
        copy(place).wait()
    last.wait()


def finish(info, labels, turns, arrived, terms):
    rows, width = terms[0].shape
    whole = pl.BlockSpec((rows, width), lambda i, *_: (0, 0))
    return pl.pallas_call(
        functools.partial(finish_kernel, turns),
        grid_spec=pltpu.PrefetchScalarGridSpec(
            num_scalar_prefetch=2,
            grid=(1,),
            in_specs=[whole] * (len(arrived) + len(terms)),
            out_specs=HBM,
            scratch_shapes=[
                pltpu.VMEM((rows, width), jnp.bfloat16),
                pltpu.SemaphoreType.DMA((len(arrived),)),
                pltpu.SemaphoreType.DMA,
            ],
        ),
        out_shape=jax.ShapeDtypeStruct((len(turns), rows, width), jnp.bfloat16),
        compiler_params=pltpu.CompilerParams(vmem_limit_bytes=GRANT),
        cost_estimate=pl.CostEstimate(
            flops=rows * width * len(terms), bytes_accessed=22 * rows * width, transcendentals=0
        ),
        name="finish",
    )(info, labels, *arrived, *terms)


def position_tables(starts, length):
    half = HEAD_DIM // 2
    frequency = ROPE_BASE ** (-jnp.arange(half, dtype=jnp.float32) / half)
    positions = starts[:, None] + jnp.arange(length, dtype=jnp.int32)[None, :]
    angles = positions.astype(jnp.float32)[..., None] * frequency
    cosine = jnp.cos(angles)
    sine = jnp.sin(angles)
    return (
        jnp.concatenate([cosine, cosine], axis=-1),
        jnp.concatenate([-sine, sine], axis=-1),
    )


def added(*terms):
    total = functools.reduce(lambda a, b: a + b, [term.astype(jnp.float32) for term in terms])
    return total.astype(jnp.bfloat16)


def paired(
    hidden, norm_gain, w_query, w_keyval, w_out, kv_cache, page_table, prefix_len, live_rows, plan
):
    groups = lax.axis_size("dp")
    group = lax.axis_index("dp")
    rank = lax.axis_index("tp")
    holding, share, _ = hidden.shape
    length = share * lax.axis_size("tp")
    limit = page_table.shape[1]
    cache = kv_cache.reshape(kv_cache.shape[0], -1, kv_cache.shape[-1])
    slot_ids = jnp.arange(holding, dtype=jnp.int32)
    info = jnp.concatenate(
        [jnp.stack([rank, group]), plan, prefix_len, live_rows, page_table.reshape(-1)]
    ).astype(jnp.int32)
    turns = list(range(groups))[::-1]
    steps = len(turns)
    sides = [(0, 1), (1, 0), (2, 3), (3, 2)]
    middle = [(1, 2), (2, 1)]
    outward = [(1, 0), (2, 3)]
    inward = [(0, 1), (3, 2)]
    is_inner = lambda r: (r == 1) | (r == 2)
    is_outer = lambda r: (r == 0) | (r == 3)
    always = lambda r: r >= 0
    block = lambda distance: lambda r: (r ^ distance) * share
    nearer = lambda r: jnp.where(is_inner(r), r ^ 3, r ^ 2) * share
    farther = lambda r: jnp.where(is_inner(r), r ^ 2, r ^ 3) * share

    (first,) = norm_some(info, turns[:1], hidden, norm_gain)
    normed = [first, *norm_some(info, turns[1:], hidden, norm_gain)]
    matches = plan[None, :] == jnp.arange(groups, dtype=jnp.int32)[:, None]
    chosen = jnp.sum(jnp.where(matches, slot_ids[None, :], 0), axis=1)
    labels = lax.all_to_all(chosen, "dp", split_axis=0, concat_axis=0, tiled=True)
    cosine, sine = position_tables(prefix_len, length)
    w_query, w_keyval = load(w_query, w_keyval, after=(labels,))
    (w_out,) = load(w_out)

    sources = []
    for step in range(steps):
        own = normed[step]
        sibling = lax.ppermute(own, "tp", sides)
        if step == 0:
            first_in = lax.ppermute(own, "tp", middle)
            second_in = lax.ppermute(sibling, "tp", middle)
            first_out = lax.ppermute(first_in, "tp", outward)
            second_out = lax.ppermute(second_in, "tp", outward)
            sources.append(
                (
                    [own, sibling, first_in, second_in, first_out, second_out],
                    [
                        (0, 0, block(0), always),
                        (1, 0, block(1), always),
                        (2, 0, block(3), is_inner),
                        (3, 0, block(2), is_inner),
                        (4, 0, block(2), is_outer),
                        (5, 0, block(3), is_outer),
                    ],
                )
            )
        else:
            pair = jnp.concatenate([own, sibling], axis=0)
            crossed = lax.ppermute(pair, "tp", middle)
            passed = lax.ppermute(crossed, "tp", outward)
            sources.append(
                (
                    [own, sibling, crossed, passed],
                    [
                        (0, 0, block(0), always),
                        (1, 0, block(1), always),
                        (2, 0, block(3), is_inner),
                        (2, 1, block(2), is_inner),
                        (3, 0, block(2), is_outer),
                        (3, 1, block(3), is_outer),
                    ],
                )
            )

    placed = None
    arrived = []
    for step, turn in enumerate(turns):
        values, places = sources[step]
        turned, kept, placed = project(
            info, turn, values, places, w_query, w_keyval, cosine, sine, placed
        )
        if step == steps - 1:
            sizes, pieces = (share,) * 4, [(d, 0, block(d)) for d in range(4)]
        else:
            sizes = (2 * share, share, share)
            pieces = [(0, 0, nearer), (0, 1, farther), (1, 0, block(1)), (2, 0, block(0))]
        parts = attend_stretch(
            info, turn, turned, kept, cache, w_out, sizes, pieces, share, holding, limit, length
        )
        if step == steps - 1:
            own, beside, beyond, across = parts
            one = lax.ppermute(across, "tp", inward)
            two = lax.ppermute(beyond, "tp", inward)
            three = lax.ppermute(beside, "tp", inward)
            four = lax.ppermute(added(beyond, one), "tp", middle)
            five = lax.ppermute(added(across, two), "tp", middle)
            six = lax.ppermute(added(beside, four), "tp", outward)
            result = finish(info, labels, turns, arrived, [own, three, five, six])
        else:
            far_part, beside, own = parts
            joined = lax.ppermute(far_part, "tp", inward)
            crossed = lax.ppermute(added(far_part, joined), "tp", middle)
            swapped = lax.ppermute(added(beside, crossed[share:]), "tp", sides)
            branch = added(own, crossed[:share], swapped)
            pairs = [(g, g ^ turn) for g in range(groups)]
            arrived.append(lax.ppermute(branch, "dp", pairs))
    return (result, placed)


def per_device(
    hidden, norm_gain, w_query, w_keyval, w_out, kv_cache, page_table, prefix_len, live_rows, plan
):
    groups = lax.axis_size("dp")
    even = groups == hidden.shape[0] == LINE
    route = paired if even and lax.axis_size("tp") == KV_HEADS == LINE else general
    return route(
        hidden, norm_gain, w_query, w_keyval, w_out, kv_cache, page_table, prefix_len, live_rows, plan
    )


def solution(mesh):
    in_specs = (
        P(("parts", "dp"), "tp", None),
        P(),
        P(None, "tp"),
        P(None, "tp"),
        P("tp", None),
        P(("parts", "dp"), "tp", None, None),
        P(("parts", "dp"), None),
        P(("parts", "dp")),
        P(("parts", "dp")),
        P(("parts", "dp")),
    )
    out_specs = (P(("parts", "dp"), "tp", None), P(("parts", "dp"), None, "tp"))
    return jax.shard_map(
        per_device, mesh=mesh, in_specs=in_specs, out_specs=out_specs, check_vma=False
    )
```

```python
import functools
import math

import jax
import jax.numpy as jnp
from jax import lax
from jax.experimental import pallas as pl
from jax.experimental.pallas import tpu as pltpu
from jax.sharding import PartitionSpec as P


KV_HEADS = 4
HEAD_DIM = 128
BLOCK = 128
MAX_PAGES = 32


EPSILON = 1e-05
ROPE_BASE = 500000.0
MASKED = -1e30
HBM = pl.BlockSpec(memory_space=pl.ANY)
GRANT = 20 << 20


def from_partner(value, axis, distance):
    mask = 2**distance
    pairs = [(source, source ^ mask) for source in range(lax.axis_size(axis))]
    return lax.ppermute(value, axis, pairs)


def rotate(values, positions):
    half_width = values.shape[-1] // 2
    frequency = ROPE_BASE ** (-jnp.arange(half_width, dtype=jnp.float32) / half_width)
    angles = positions.astype(jnp.float32)[..., None] * frequency
    cosine = jnp.cos(angles)[..., None, :]
    sine_values = jnp.sin(angles)[..., None, :]
    front_half = values[..., :half_width]
    back_half = values[..., half_width:]
    return jnp.concatenate(
        [
            front_half * cosine - back_half * sine_values,
            back_half * cosine + front_half * sine_values,
        ],
        axis=-1,
    )


def attend_one(inputs):
    queries, head_pairs, prefix, start, count = inputs
    head_width = queries.shape[-1]
    scaling = 1.0 / math.sqrt(head_width)
    row_count = queries.shape[0]
    row_index = jnp.arange(row_count, dtype=jnp.int32)
    own_mask = (row_index[None, :] <= row_index[:, None]) & (row_index[None, :] < count)
    own_scores = (
        jnp.einsum(
            "chd,jd->hcj", queries, head_pairs[:, :head_width], preferred_element_type=jnp.float32
        )
        * scaling
    )
    own_scores = jnp.where(own_mask[None], own_scores, MASKED)
    span_pages = max(1, min(MAX_PAGES, 512 // BLOCK))
    key_span = span_pages * BLOCK
    block_count = (start + key_span - 1) // key_span

    def block_scores(block_id):
        key_block = lax.dynamic_slice_in_dim(prefix, block_id * key_span, key_span, 0)
        scores = (
            jnp.einsum(
                "chd,td->hct",
                queries,
                key_block[:, :head_width],
                preferred_element_type=jnp.float32,
            )
            * scaling
        )
        key_place = block_id * key_span + jnp.arange(key_span, dtype=jnp.int32)
        key_mask = key_place < start
        return (jnp.where(key_mask[None, None, :], scores, MASKED), key_block)

    running_max = jnp.max(own_scores, axis=-1)
    running_sum = jnp.sum(jnp.exp(own_scores - running_max[..., None]), axis=-1)

    def first_pass(block_id, state_pair):
        old_max, old_sum = state_pair
        scores, _ = block_scores(block_id)
        raised_max = jnp.maximum(old_max, jnp.max(scores, axis=-1))
        new_sum = old_sum * jnp.exp(old_max - raised_max) + jnp.sum(
            jnp.exp(scores - raised_max[..., None]), axis=-1
        )
        return (raised_max, new_sum)

    running_max, running_sum = lax.fori_loop(0, block_count, first_pass, (running_max, running_sum))

    def normalize(scores):
        return (jnp.exp(scores - running_max[..., None]) / running_sum[..., None]).astype(
            jnp.bfloat16
        )

    attended = jnp.einsum(
        "hcj,jd->chd",
        normalize(own_scores),
        head_pairs[:, head_width:],
        preferred_element_type=jnp.float32,
    )

    def second_pass(block_id, gathered_sum):
        scores, key_block = block_scores(block_id)
        return gathered_sum + jnp.einsum(
            "hct,td->chd",
            normalize(scores),
            key_block[:, head_width:],
            preferred_element_type=jnp.float32,
        )

    attended = lax.fori_loop(0, block_count, second_pass, attended)
    return attended.astype(jnp.bfloat16)


def attend(queries, head_pairs, prefix, starts, counts):
    return lax.map(attend_one, (queries, head_pairs, prefix, starts, counts))


def layer(stretch_rows, stretch_pages, starts, counts, norm_gain, w_query, w_keyval, w_out):
    tensor_size = lax.axis_size("tp")
    tensor_rank = lax.axis_index("tp")
    widened = stretch_rows.astype(jnp.float32)
    normed = (
        widened
        * lax.rsqrt(jnp.mean(widened * widened, axis=-1, keepdims=True) + EPSILON)
        * norm_gain.astype(jnp.float32)
    ).astype(jnp.bfloat16)
    query_width = w_query.shape[1]
    portion = lax.all_gather(normed, "tp", axis=1, tiled=True)
    query_part = jnp.einsum("ocd,dk->ock", portion, w_query, preferred_element_type=jnp.float32)
    pair_part = jnp.einsum("ocd,dk->ock", portion, w_keyval, preferred_element_type=jnp.float32)
    projected = jnp.concatenate([query_part, pair_part], axis=-1)
    holding = projected.shape[0]
    length = projected.shape[1]
    head_width = HEAD_DIM
    positions = starts[:, None] + jnp.arange(length, dtype=jnp.int32)[None, :]
    queries = rotate(
        projected[..., :query_width].reshape(
            holding, length, query_width // head_width, head_width
        ),
        positions,
    ).astype(jnp.bfloat16)
    pair_piece = projected[..., query_width:].astype(jnp.bfloat16)
    sharers = tensor_size // KV_HEADS
    levels = sharers.bit_length() - 1
    sharer_rank = tensor_rank % sharers
    page_piece = stretch_pages
    for level_bit in range(levels):
        their_pairs, their_pages = from_partner((pair_piece, page_piece), "tp", level_bit)
        upper_half = tensor_rank // (1 << level_bit) % 2 == 1
        pair_piece = jnp.where(
            upper_half,
            jnp.concatenate([their_pairs, pair_piece], axis=-1),
            jnp.concatenate([pair_piece, their_pairs], axis=-1),
        )
        page_piece = jnp.where(
            upper_half,
            jnp.concatenate([their_pages, page_piece], axis=2),
            jnp.concatenate([page_piece, their_pages], axis=2),
        )
    live_mask = jnp.arange(length, dtype=jnp.int32)[None, :] < counts[:, None]
    rotated_keys = rotate(
        pair_piece[..., :head_width].astype(jnp.float32)[:, :, None, :], positions
    )[:, :, 0, :]
    head_pairs = (
        jnp.concatenate([rotated_keys, pair_piece[..., head_width:].astype(jnp.float32)], axis=-1)
        * live_mask[..., None].astype(jnp.float32)
    ).astype(jnp.bfloat16)
    piece_width = 2 * head_width // sharers
    columns = lax.dynamic_slice_in_dim(head_pairs, sharer_rank * piece_width, piece_width, 2)
    prefix = page_piece.reshape(holding, -1, 2 * head_width)
    attended = attend(queries, head_pairs, prefix, starts, counts)
    partial_value = jnp.einsum(
        "ock,kd->ocd",
        attended.reshape(holding, length, -1),
        w_out,
        preferred_element_type=jnp.float32,
    )
    summed = lax.psum_scatter(
        partial_value.astype(jnp.bfloat16), "tp", scatter_dimension=1, tiled=True
    ).astype(jnp.float32)
    share_rows = summed.shape[1]
    row_ids = tensor_rank * share_rows + jnp.arange(share_rows, dtype=jnp.int32)
    keep_rows = row_ids[None, :] < counts[:, None]
    result = jnp.where(keep_rows[..., None], summed, jnp.zeros_like(summed)).astype(jnp.bfloat16)
    return (result, columns)


def general(
    hidden, norm_gain, w_query, w_keyval, w_out, kv_cache, page_table, prefix_len, live_rows, plan
):
    groups = lax.axis_size("dp")
    holding = hidden.shape[0]
    slot_ids = jnp.arange(holding, dtype=jnp.int32)
    gathered_pages = kv_cache[page_table]
    target = jnp.arange(groups, dtype=jnp.int32)
    matches = plan[None, :] == target[:, None]
    present = jnp.any(matches, axis=1)
    chosen = jnp.argmax(matches, axis=1)
    labels = jnp.where(present, chosen, -1)
    local_rows, new_kv = layer(
        hidden, gathered_pages, prefix_len, live_rows, norm_gain, w_query, w_keyval, w_out
    )
    outgoing = jnp.where(
        present[:, None, None], local_rows[chosen], jnp.zeros((), local_rows.dtype)
    )
    arrived, labels_arrived = (
        lax.all_to_all(outgoing, "dp", split_axis=0, concat_axis=0, tiled=True),
        lax.all_to_all(labels, "dp", split_axis=0, concat_axis=0, tiled=True),
    )
    source = jnp.argmax(labels_arrived[None, :] == slot_ids[:, None], axis=1)
    result = arrived[source]
    return (result, new_kv)


LINE = 4
CHUNK = 128
GROUP = 4


def pick_of(info_ref, turn, holding):
    target = info_ref[1] ^ turn
    pick = 0
    for place in range(1, holding):
        pick = jnp.where(info_ref[2 + place] == target, place, pick)
    return pick


def norm_kernel(info_ref, hidden_ref, gain_ref, *out_refs):
    step = pl.program_id(0)
    widened = hidden_ref[0].astype(jnp.float32)
    mean = jnp.mean(widened * widened, axis=-1, keepdims=True)
    gain = gain_ref[...].astype(jnp.float32)[None, :]
    normed = (widened * lax.rsqrt(mean + EPSILON) * gain).astype(jnp.bfloat16)
    for place, out_ref in enumerate(out_refs):
        @pl.when(step == place)
        def _():
            out_ref[...] = normed


def norm_some(info, turns, hidden, gain):
    holding, rows, width = hidden.shape

    def chosen(i, info_ref):
        turn = jnp.int32(turns[0])
        for place in range(1, len(turns)):
            turn = jnp.where(i == place, turns[place], turn)
        return (pick_of(info_ref, turn, holding), 0, 0)

    return pl.pallas_call(
        norm_kernel,
        grid_spec=pltpu.PrefetchScalarGridSpec(
            num_scalar_prefetch=1,
            grid=(len(turns),),
            in_specs=[
                pl.BlockSpec((1, rows, width), chosen),
                pl.BlockSpec((width,), lambda i, info_ref: (0,)),
            ],
            out_specs=[pl.BlockSpec((rows, width), lambda i, info_ref: (0, 0))] * len(turns),
        ),
        out_shape=[jax.ShapeDtypeStruct((rows, width), jnp.bfloat16)] * len(turns),
        compiler_params=pltpu.CompilerParams(vmem_limit_bytes=GRANT),
        cost_estimate=pl.CostEstimate(
            flops=4 * rows * width * len(turns),
            bytes_accessed=4 * rows * width * len(turns),
            transcendentals=rows,
        ),
        name="norm_some",
    )(info, hidden, gain)


def load_kernel(count, *refs):
    sources, kept, sems = refs[:count], refs[-1 - count : -1], refs[-1]
    copies = [
        pltpu.make_async_copy(sources[place], kept[place], sems.at[place]) for place in range(count)
    ]
    for item in copies:
        item.start()
    for item in copies:
        item.wait()


def load(*arrays, after=()):
    kept = pl.BlockSpec(memory_space=pltpu.MemorySpace.VMEM)
    return pl.pallas_call(
        functools.partial(load_kernel, len(arrays)),
        in_specs=[HBM] * (len(arrays) + len(after)),
        out_specs=[kept] * len(arrays),
        out_shape=[pltpu.VMEM(item.shape, item.dtype) for item in arrays],
        scratch_shapes=[pltpu.SemaphoreType.DMA((len(arrays),))],
        compiler_params=pltpu.CompilerParams(vmem_limit_bytes=GRANT),
        name="load",
    )(*stored_of(*arrays), *after)


def stored_of(*arrays):
    return [pltpu.with_memory_space_constraint(item, pltpu.MemorySpace.HBM) for item in arrays]


def resident_of(*arrays):
    return [pltpu.with_memory_space_constraint(item, pltpu.MemorySpace.VMEM) for item in arrays]


def project_kernel(count, share, places, turn, holding, head_width, tile, aliased, info_ref, *refs):
    sources = refs[:count]
    query_ref, pair_ref, cosine_ref, sine_ref = refs[count : count + 4]
    refs = refs[count + 4 + aliased :]
    turned_ref, kept_ref, placed_ref = refs[:3]
    rows_ref, sems = refs[3:]
    wide = query_ref.shape[1]
    rank = info_ref[0]
    live = info_ref[2 + 2 * holding + pick_of(info_ref, turn, holding)]

    def copy(place):
        source, half = places[place][:2]
        start = pl.multiple_of(places[place][2](rank), share)
        return pltpu.make_async_copy(
            sources[source].at[pl.ds(half * share, share)],
            rows_ref.at[pl.ds(start, share)],
            sems.at[place],
        )

    for place in range(len(places)):
        @pl.when(places[place][3](rank))
        def _():
            copy(place).start()
    for place in range(len(places)):
        @pl.when(places[place][3](rank))
        def _():
            copy(place).wait()

    length = rows_ref.shape[0]
    cosine = cosine_ref[0]
    sine = sine_ref[0]
    half = head_width // 2

    def turn_rows(values):
        return values * cosine + pltpu.roll(values, half, 1) * sine

    @pl.loop(0, wide // tile)
    def _(step):
        span = pl.ds(pl.multiple_of(step * tile, tile), tile)
        part = jnp.dot(rows_ref[...], query_ref[:, span], preferred_element_type=jnp.float32)
        for head in range(tile // head_width):
            turned = turn_rows(part[:, head * head_width : (head + 1) * head_width])
            place = pl.ds(pl.multiple_of((step * (tile // head_width) + head) * length, length), length)
            turned_ref[:, place] = turned.T.astype(turned_ref.dtype)

    pairs = jnp.dot(rows_ref[...], pair_ref[...], preferred_element_type=jnp.float32)
    pairs = pairs.astype(jnp.bfloat16).astype(jnp.float32)
    keys, values = pairs[:, :head_width], pairs[:, head_width:]
    row = lax.broadcasted_iota(jnp.int32, keys.shape, 0)
    keys = jnp.where(row < live, turn_rows(keys), 0.0).astype(kept_ref.dtype)
    values = jnp.where(row < live, values, 0.0).astype(kept_ref.dtype)
    for target in (kept_ref, placed_ref.at[0]):
        target[:, :head_width] = keys
        target[:, head_width:] = values


def project(info, turn, sources, places, w_query, w_keyval, cosine, sine, placed):
    share = sources[0].shape[0]
    width, wide = w_query.shape
    narrow = w_keyval.shape[1]
    holding, length, head_width = cosine.shape
    tile = min(wide, 2 * head_width)
    resident = pl.BlockSpec(memory_space=pltpu.MemorySpace.VMEM)
    picked = lambda i, info_ref: (pick_of(info_ref, turn, holding), 0, 0)
    fixed = lambda i, info_ref: (0, 0)
    lanes = wide // head_width * length
    extra = [] if placed is None else [placed]
    return pl.pallas_call(
        functools.partial(
            project_kernel, len(sources), share, places, turn, holding, head_width, tile, len(extra)
        ),
        grid_spec=pltpu.PrefetchScalarGridSpec(
            num_scalar_prefetch=1,
            grid=(1,),
            in_specs=[HBM] * len(sources)
            + [resident] * 2
            + [pl.BlockSpec((1, length, head_width), picked)] * 2
            + [HBM] * len(extra),
            out_specs=[
                pl.BlockSpec((head_width, lanes), fixed),
                pl.BlockSpec((length, narrow), fixed),
                pl.BlockSpec((1, length, narrow), picked),
            ],
            scratch_shapes=[
                pltpu.VMEM((length, width), jnp.bfloat16),
                pltpu.SemaphoreType.DMA((len(places),)),
            ],
        ),
        out_shape=[
            jax.ShapeDtypeStruct((head_width, lanes), jnp.bfloat16),
            jax.ShapeDtypeStruct((length, narrow), jnp.bfloat16),
            jax.ShapeDtypeStruct((holding, length, narrow), jnp.bfloat16),
        ],
        input_output_aliases={len(sources) + 5: 2} if extra else {},
        compiler_params=pltpu.CompilerParams(vmem_limit_bytes=GRANT),
        cost_estimate=pl.CostEstimate(
            flops=2 * length * width * (wide + narrow),
            bytes_accessed=2 * length * width,
            transcendentals=0,
        ),
        name="project",
    )(info, *stored_of(*sources), *resident_of(w_query, w_keyval), cosine, sine, *extra)


def stretch_kernel(
    count, part, pieces, turn, holding, limit, length, group, tile, info_ref, turned_ref, kept_ref, cache_ref, out_w_ref, *refs
):
    outs = refs[:count]
    stored, product, heads_ref, top_ref, sum_ref, acc_ref, page_sems, out_sems = refs[count:]
    block = cache_ref.shape[1]
    head_width = kept_ref.shape[1] // 2
    lanes = turned_ref.shape[1]
    rank = info_ref[0]
    pick = pick_of(info_ref, turn, holding)
    pages = info_ref[2 + holding + pick] // block
    live = info_ref[2 + 2 * holding + pick]
    base = 2 + 3 * holding + pick * limit
    tiles = product.shape[0]
    scale = (1.0 / math.sqrt(head_width)) * math.log2(math.e)

    def page_copy(place):
        start = pl.multiple_of(place * block, block)
        return pltpu.make_async_copy(
            cache_ref.at[info_ref[base + place]], stored.at[pl.ds(start, block)], page_sems.at[place]
        )

    @pl.loop(0, pages)
    def _(place):
        page_copy(place).start()

    def fold(keys, values, mask):
        for first in range(0, lanes, chunk):
            span = slice(first, first + chunk)
            scores = jnp.dot(keys, turned_ref[:, span], preferred_element_type=jnp.float32)
            if mask is not None:
                scores = jnp.where(mask, scores, MASKED)
                top = jnp.max(scores, axis=0, keepdims=True)
            else:
                top = jnp.maximum(top_ref[:, span], jnp.max(scores, axis=0, keepdims=True))
            exps = jnp.exp2((scores - top) * scale)
            summed = jnp.sum(exps, axis=0, keepdims=True)
            taken = lax.dot_general(
                values, exps.astype(jnp.bfloat16), (((0,), (0,)), ((), ())), preferred_element_type=jnp.float32
            )
            if mask is not None:
                sum_ref[:, span] = summed
                acc_ref[:, span] = taken
            else:
                fade = jnp.exp2((top_ref[:, span] - top) * scale)
                sum_ref[:, span] = sum_ref[:, span] * fade + summed
                acc_ref[:, span] = acc_ref[:, span] * fade + taken
            top_ref[:, span] = top

    chunk = min(lanes, CHUNK)
    key_row = lax.broadcasted_iota(jnp.int32, (length, chunk), 0)
    query_row = lax.rem(lax.broadcasted_iota(jnp.int32, (length, chunk), 1), length)
    fold(kept_ref[:, :head_width], kept_ref[:, head_width:], (key_row <= query_row) & (key_row < live))

    def fold_span(first, span):
        for item in range(span):
            page_copy(first + item).wait()
        rows = pl.ds(pl.multiple_of(first * block, block), span * block)
        fold(stored[rows, :head_width], stored[rows, head_width:], None)

    whole = pages // group

    @pl.loop(0, whole)
    def _(step):
        fold_span(step * group, group)

    @pl.loop(whole * group, pages)
    def _(place):
        fold_span(place, 1)

    share = acc_ref[...] / sum_ref[...]
    row = lax.broadcasted_iota(jnp.int32, (length, head_width), 0)
    for head in range(lanes // length):
        span = slice(head * length, (head + 1) * length)
        heads_ref[:, head * head_width : (head + 1) * head_width] = jnp.where(
            row < live, share[:, span].T, 0.0
        ).astype(heads_ref.dtype)

    def out_copies(place):
        copies = []
        for item, (out, half, row_start) in enumerate(pieces):
            start = pl.multiple_of(row_start(rank), part)
            columns = pl.ds(pl.multiple_of(place * tile, tile), tile)
            copies.append(
                pltpu.make_async_copy(
                    product.at[place, pl.ds(start, part)],
                    outs[out].at[pl.ds(half * part, part), columns],
                    out_sems.at[item, place],
                )
            )
        return copies

    @pl.loop(0, tiles)
    def _(place):
        columns = pl.ds(pl.multiple_of(place * tile, tile), tile)
        product[place] = jnp.dot(
            heads_ref[...], out_w_ref[:, columns], preferred_element_type=jnp.float32
        ).astype(product.dtype)
        for item in out_copies(place):
            item.start()

    @pl.loop(0, tiles)
    def _(place):
        for item in out_copies(place):
            item.wait()


def attend_stretch(info, turn, turned, kept, cache, w_out, sizes, pieces, part, holding, limit, length):
    head_width, lanes = turned.shape
    block = cache.shape[1]
    inner, width = w_out.shape
    tile = min(width, 1024)
    tiles = width // tile
    group = min(GROUP, limit)
    return pl.pallas_call(
        functools.partial(
            stretch_kernel, len(sizes), part, pieces, turn, holding, limit, length, group, tile
        ),
        grid_spec=pltpu.PrefetchScalarGridSpec(
            num_scalar_prefetch=1,
            grid=(1,),
            in_specs=[
                pl.BlockSpec(turned.shape, lambda i, info_ref: (0, 0)),
                pl.BlockSpec(kept.shape, lambda i, info_ref: (0, 0)),
                HBM,
                pl.BlockSpec(memory_space=pltpu.MemorySpace.VMEM),
            ],
            out_specs=[HBM] * len(sizes),
            scratch_shapes=[
                pltpu.VMEM((limit * block, 2 * head_width), jnp.bfloat16),
                pltpu.VMEM((tiles, length, tile), jnp.bfloat16),
                pltpu.VMEM((length, inner), jnp.bfloat16),
                pltpu.VMEM((1, lanes), jnp.float32),
                pltpu.VMEM((1, lanes), jnp.float32),
                pltpu.VMEM((head_width, lanes), jnp.float32),
                pltpu.SemaphoreType.DMA((limit,)),
                pltpu.SemaphoreType.DMA((len(pieces), tiles)),
            ],
        ),
        out_shape=[jax.ShapeDtypeStruct((size, width), jnp.bfloat16) for size in sizes],
        compiler_params=pltpu.CompilerParams(vmem_limit_bytes=GRANT),
        cost_estimate=pl.CostEstimate(
            flops=4 * lanes * head_width * limit * block + 2 * length * inner * width,
            bytes_accessed=4 * limit * block * head_width,
            transcendentals=lanes * limit * block,
        ),
        name="attend",
    )(info, turned, kept, *stored_of(cache), *resident_of(w_out))


def finish_kernel(turns, info_ref, labels_ref, *refs):
    count = len(turns) - 1
    moved_refs, terms = refs[:count], refs[count:-4]
    out_ref, last_ref, sems, last_sem = refs[-4:]
    group = info_ref[1]

    def copy(place):
        return pltpu.make_async_copy(
            moved_refs[place], out_ref.at[labels_ref[group ^ turns[place]]], sems.at[place]
        )

    for place in range(count):
        copy(place).start()
    total = terms[0][...].astype(jnp.float32)
    for term in terms[1:]:
        total += term[...].astype(jnp.float32)
    last_ref[...] = total.astype(last_ref.dtype)
    last = pltpu.make_async_copy(last_ref, out_ref.at[labels_ref[group ^ turns[count]]], last_sem)
    last.start()
    for place in range(count):
        copy(place).wait()
    last.wait()


def finish(info, labels, turns, arrived, terms):
    rows, width = terms[0].shape
    whole = pl.BlockSpec((rows, width), lambda i, *_: (0, 0))
    return pl.pallas_call(
        functools.partial(finish_kernel, turns),
        grid_spec=pltpu.PrefetchScalarGridSpec(
            num_scalar_prefetch=2,
            grid=(1,),
            in_specs=[whole] * (len(arrived) + len(terms)),
            out_specs=HBM,
            scratch_shapes=[
                pltpu.VMEM((rows, width), jnp.bfloat16),
                pltpu.SemaphoreType.DMA((len(arrived),)),
                pltpu.SemaphoreType.DMA,
            ],
        ),
        out_shape=jax.ShapeDtypeStruct((len(turns), rows, width), jnp.bfloat16),
        compiler_params=pltpu.CompilerParams(vmem_limit_bytes=GRANT),
        cost_estimate=pl.CostEstimate(
            flops=rows * width * len(terms), bytes_accessed=22 * rows * width, transcendentals=0
        ),
        name="finish",
    )(info, labels, *arrived, *terms)


def position_tables(starts, length):
    half = HEAD_DIM // 2
    frequency = ROPE_BASE ** (-jnp.arange(half, dtype=jnp.float32) / half)
    positions = starts[:, None] + jnp.arange(length, dtype=jnp.int32)[None, :]
    angles = positions.astype(jnp.float32)[..., None] * frequency
    cosine = jnp.cos(angles)
    sine = jnp.sin(angles)
    return (
        jnp.concatenate([cosine, cosine], axis=-1),
        jnp.concatenate([-sine, sine], axis=-1),
    )


def added(*terms):
    total = functools.reduce(lambda a, b: a + b, [term.astype(jnp.float32) for term in terms])
    return total.astype(jnp.bfloat16)


def paired(
    hidden, norm_gain, w_query, w_keyval, w_out, kv_cache, page_table, prefix_len, live_rows, plan
):
    groups = lax.axis_size("dp")
    group = lax.axis_index("dp")
    rank = lax.axis_index("tp")
    holding, share, _ = hidden.shape
    length = share * lax.axis_size("tp")
    limit = page_table.shape[1]
    cache = kv_cache.reshape(kv_cache.shape[0], -1, kv_cache.shape[-1])
    slot_ids = jnp.arange(holding, dtype=jnp.int32)
    info = jnp.concatenate(
        [jnp.stack([rank, group]), plan, prefix_len, live_rows, page_table.reshape(-1)]
    ).astype(jnp.int32)
    turns = list(range(groups))[::-1]
    steps = len(turns)
    sides = [(0, 1), (1, 0), (2, 3), (3, 2)]
    middle = [(1, 2), (2, 1)]
    outward = [(1, 0), (2, 3)]
    inward = [(0, 1), (3, 2)]
    is_inner = lambda r: (r == 1) | (r == 2)
    is_outer = lambda r: (r == 0) | (r == 3)
    always = lambda r: r >= 0
    block = lambda distance: lambda r: (r ^ distance) * share
    nearer = lambda r: jnp.where(is_inner(r), r ^ 3, r ^ 2) * share
    farther = lambda r: jnp.where(is_inner(r), r ^ 2, r ^ 3) * share

    (first,) = norm_some(info, turns[:1], hidden, norm_gain)
    normed = [first, *norm_some(info, turns[1:], hidden, norm_gain)]
    matches = plan[None, :] == jnp.arange(groups, dtype=jnp.int32)[:, None]
    chosen = jnp.sum(jnp.where(matches, slot_ids[None, :], 0), axis=1)
    labels = lax.all_to_all(chosen, "dp", split_axis=0, concat_axis=0, tiled=True)
    cosine, sine = position_tables(prefix_len, length)
    w_query, w_keyval = load(w_query, w_keyval, after=(labels,))
    (w_out,) = load(w_out)

    sources = []
    for step in range(steps):
        own = normed[step]
        sibling = lax.ppermute(own, "tp", sides)
        if step == 0:
            first_in = lax.ppermute(own, "tp", middle)
            second_in = lax.ppermute(sibling, "tp", middle)
            first_out = lax.ppermute(first_in, "tp", outward)
            second_out = lax.ppermute(second_in, "tp", outward)
            sources.append(
                (
                    [own, sibling, first_in, second_in, first_out, second_out],
                    [
                        (0, 0, block(0), always),
                        (1, 0, block(1), always),
                        (2, 0, block(3), is_inner),
                        (3, 0, block(2), is_inner),
                        (4, 0, block(2), is_outer),
                        (5, 0, block(3), is_outer),
                    ],
                )
            )
        else:
            pair = jnp.concatenate([own, sibling], axis=0)
            crossed = lax.ppermute(pair, "tp", middle)
            passed = lax.ppermute(crossed, "tp", outward)
            sources.append(
                (
                    [own, sibling, crossed, passed],
                    [
                        (0, 0, block(0), always),
                        (1, 0, block(1), always),
                        (2, 0, block(3), is_inner),
                        (2, 1, block(2), is_inner),
                        (3, 0, block(2), is_outer),
                        (3, 1, block(3), is_outer),
                    ],
                )
            )

    placed = None
    arrived = []
    for step, turn in enumerate(turns):
        values, places = sources[step]
        turned, kept, placed = project(
            info, turn, values, places, w_query, w_keyval, cosine, sine, placed
        )
        if step == steps - 1:
            sizes, pieces = (share,) * 4, [(d, 0, block(d)) for d in range(4)]
        else:
            sizes = (2 * share, share, share)
            pieces = [(0, 0, nearer), (0, 1, farther), (1, 0, block(1)), (2, 0, block(0))]
        parts = attend_stretch(
            info, turn, turned, kept, cache, w_out, sizes, pieces, share, holding, limit, length
        )
        if step == steps - 1:
            own, beside, beyond, across = parts
            one = lax.ppermute(across, "tp", inward)
            two = lax.ppermute(beyond, "tp", inward)
            three = lax.ppermute(beside, "tp", inward)
            four = lax.ppermute(added(beyond, one), "tp", middle)
            five = lax.ppermute(added(across, two), "tp", middle)
            six = lax.ppermute(added(beside, four), "tp", outward)
            result = finish(info, labels, turns, arrived, [own, three, five, six])
        else:
            far_part, beside, own = parts
            joined = lax.ppermute(far_part, "tp", inward)
            crossed = lax.ppermute(added(far_part, joined), "tp", middle)
            from_outer = lax.ppermute(beside, "tp", inward)
            outgoing = added(beside, crossed[share:])
            from_inner = lax.ppermute(outgoing, "tp", outward)
            branch = added(own, crossed[:share], from_outer, from_inner)
            pairs = [(g, g ^ turn) for g in range(groups)]
            arrived.append(lax.ppermute(branch, "dp", pairs))
    return (result, placed)


def per_device(
    hidden, norm_gain, w_query, w_keyval, w_out, kv_cache, page_table, prefix_len, live_rows, plan
):
    groups = lax.axis_size("dp")
    even = groups == hidden.shape[0] == LINE
    route = paired if even and lax.axis_size("tp") == KV_HEADS == LINE else general
    return route(
        hidden, norm_gain, w_query, w_keyval, w_out, kv_cache, page_table, prefix_len, live_rows, plan
    )


def solution(mesh):
    in_specs = (
        P(("parts", "dp"), "tp", None),
        P(),
        P(None, "tp"),
        P(None, "tp"),
        P("tp", None),
        P(("parts", "dp"), "tp", None, None),
        P(("parts", "dp"), None),
        P(("parts", "dp")),
        P(("parts", "dp")),
        P(("parts", "dp")),
    )
    out_specs = (P(("parts", "dp"), "tp", None), P(("parts", "dp"), None, "tp"))
    return jax.shard_map(
        per_device, mesh=mesh, in_specs=in_specs, out_specs=out_specs, check_vma=False
    )
```

```python
import functools
import math

import jax
import jax.numpy as jnp
from jax import lax
from jax.experimental import pallas as pl
from jax.experimental.pallas import tpu as pltpu
from jax.sharding import PartitionSpec as P


KV_HEADS = 4
HEAD_DIM = 128
BLOCK = 128
MAX_PAGES = 32


EPSILON = 1e-05
ROPE_BASE = 500000.0
MASKED = -1e30
HBM = pl.BlockSpec(memory_space=pl.ANY)
GRANT = 20 << 20


def from_partner(value, axis, distance):
    mask = 2**distance
    pairs = [(source, source ^ mask) for source in range(lax.axis_size(axis))]
    return lax.ppermute(value, axis, pairs)


def rotate(values, positions):
    half_width = values.shape[-1] // 2
    frequency = ROPE_BASE ** (-jnp.arange(half_width, dtype=jnp.float32) / half_width)
    angles = positions.astype(jnp.float32)[..., None] * frequency
    cosine = jnp.cos(angles)[..., None, :]
    sine_values = jnp.sin(angles)[..., None, :]
    front_half = values[..., :half_width]
    back_half = values[..., half_width:]
    return jnp.concatenate(
        [
            front_half * cosine - back_half * sine_values,
            back_half * cosine + front_half * sine_values,
        ],
        axis=-1,
    )


def attend_one(inputs):
    queries, head_pairs, prefix, start, count = inputs
    head_width = queries.shape[-1]
    scaling = 1.0 / math.sqrt(head_width)
    row_count = queries.shape[0]
    row_index = jnp.arange(row_count, dtype=jnp.int32)
    own_mask = (row_index[None, :] <= row_index[:, None]) & (row_index[None, :] < count)
    own_scores = (
        jnp.einsum(
            "chd,jd->hcj", queries, head_pairs[:, :head_width], preferred_element_type=jnp.float32
        )
        * scaling
    )
    own_scores = jnp.where(own_mask[None], own_scores, MASKED)
    span_pages = max(1, min(MAX_PAGES, 512 // BLOCK))
    key_span = span_pages * BLOCK
    block_count = (start + key_span - 1) // key_span

    def block_scores(block_id):
        key_block = lax.dynamic_slice_in_dim(prefix, block_id * key_span, key_span, 0)
        scores = (
            jnp.einsum(
                "chd,td->hct",
                queries,
                key_block[:, :head_width],
                preferred_element_type=jnp.float32,
            )
            * scaling
        )
        key_place = block_id * key_span + jnp.arange(key_span, dtype=jnp.int32)
        key_mask = key_place < start
        return (jnp.where(key_mask[None, None, :], scores, MASKED), key_block)

    running_max = jnp.max(own_scores, axis=-1)
    running_sum = jnp.sum(jnp.exp(own_scores - running_max[..., None]), axis=-1)

    def first_pass(block_id, state_pair):
        old_max, old_sum = state_pair
        scores, _ = block_scores(block_id)
        raised_max = jnp.maximum(old_max, jnp.max(scores, axis=-1))
        new_sum = old_sum * jnp.exp(old_max - raised_max) + jnp.sum(
            jnp.exp(scores - raised_max[..., None]), axis=-1
        )
        return (raised_max, new_sum)

    running_max, running_sum = lax.fori_loop(0, block_count, first_pass, (running_max, running_sum))

    def normalize(scores):
        return (jnp.exp(scores - running_max[..., None]) / running_sum[..., None]).astype(
            jnp.bfloat16
        )

    attended = jnp.einsum(
        "hcj,jd->chd",
        normalize(own_scores),
        head_pairs[:, head_width:],
        preferred_element_type=jnp.float32,
    )

    def second_pass(block_id, gathered_sum):
        scores, key_block = block_scores(block_id)
        return gathered_sum + jnp.einsum(
            "hct,td->chd",
            normalize(scores),
            key_block[:, head_width:],
            preferred_element_type=jnp.float32,
        )

    attended = lax.fori_loop(0, block_count, second_pass, attended)
    return attended.astype(jnp.bfloat16)


def attend(queries, head_pairs, prefix, starts, counts):
    return lax.map(attend_one, (queries, head_pairs, prefix, starts, counts))


def layer(stretch_rows, stretch_pages, starts, counts, norm_gain, w_query, w_keyval, w_out):
    tensor_size = lax.axis_size("tp")
    tensor_rank = lax.axis_index("tp")
    widened = stretch_rows.astype(jnp.float32)
    normed = (
        widened
        * lax.rsqrt(jnp.mean(widened * widened, axis=-1, keepdims=True) + EPSILON)
        * norm_gain.astype(jnp.float32)
    ).astype(jnp.bfloat16)
    query_width = w_query.shape[1]
    portion = lax.all_gather(normed, "tp", axis=1, tiled=True)
    query_part = jnp.einsum("ocd,dk->ock", portion, w_query, preferred_element_type=jnp.float32)
    pair_part = jnp.einsum("ocd,dk->ock", portion, w_keyval, preferred_element_type=jnp.float32)
    projected = jnp.concatenate([query_part, pair_part], axis=-1)
    holding = projected.shape[0]
    length = projected.shape[1]
    head_width = HEAD_DIM
    positions = starts[:, None] + jnp.arange(length, dtype=jnp.int32)[None, :]
    queries = rotate(
        projected[..., :query_width].reshape(
            holding, length, query_width // head_width, head_width
        ),
        positions,
    ).astype(jnp.bfloat16)
    pair_piece = projected[..., query_width:].astype(jnp.bfloat16)
    sharers = tensor_size // KV_HEADS
    levels = sharers.bit_length() - 1
    sharer_rank = tensor_rank % sharers
    page_piece = stretch_pages
    for level_bit in range(levels):
        their_pairs, their_pages = from_partner((pair_piece, page_piece), "tp", level_bit)
        upper_half = tensor_rank // (1 << level_bit) % 2 == 1
        pair_piece = jnp.where(
            upper_half,
            jnp.concatenate([their_pairs, pair_piece], axis=-1),
            jnp.concatenate([pair_piece, their_pairs], axis=-1),
        )
        page_piece = jnp.where(
            upper_half,
            jnp.concatenate([their_pages, page_piece], axis=2),
            jnp.concatenate([page_piece, their_pages], axis=2),
        )
    live_mask = jnp.arange(length, dtype=jnp.int32)[None, :] < counts[:, None]
    rotated_keys = rotate(
        pair_piece[..., :head_width].astype(jnp.float32)[:, :, None, :], positions
    )[:, :, 0, :]
    head_pairs = (
        jnp.concatenate([rotated_keys, pair_piece[..., head_width:].astype(jnp.float32)], axis=-1)
        * live_mask[..., None].astype(jnp.float32)
    ).astype(jnp.bfloat16)
    piece_width = 2 * head_width // sharers
    columns = lax.dynamic_slice_in_dim(head_pairs, sharer_rank * piece_width, piece_width, 2)
    prefix = page_piece.reshape(holding, -1, 2 * head_width)
    attended = attend(queries, head_pairs, prefix, starts, counts)
    partial_value = jnp.einsum(
        "ock,kd->ocd",
        attended.reshape(holding, length, -1),
        w_out,
        preferred_element_type=jnp.float32,
    )
    summed = lax.psum_scatter(
        partial_value.astype(jnp.bfloat16), "tp", scatter_dimension=1, tiled=True
    ).astype(jnp.float32)
    share_rows = summed.shape[1]
    row_ids = tensor_rank * share_rows + jnp.arange(share_rows, dtype=jnp.int32)
    keep_rows = row_ids[None, :] < counts[:, None]
    result = jnp.where(keep_rows[..., None], summed, jnp.zeros_like(summed)).astype(jnp.bfloat16)
    return (result, columns)


def general(
    hidden, norm_gain, w_query, w_keyval, w_out, kv_cache, page_table, prefix_len, live_rows, plan
):
    groups = lax.axis_size("dp")
    holding = hidden.shape[0]
    slot_ids = jnp.arange(holding, dtype=jnp.int32)
    gathered_pages = kv_cache[page_table]
    target = jnp.arange(groups, dtype=jnp.int32)
    matches = plan[None, :] == target[:, None]
    present = jnp.any(matches, axis=1)
    chosen = jnp.argmax(matches, axis=1)
    labels = jnp.where(present, chosen, -1)
    local_rows, new_kv = layer(
        hidden, gathered_pages, prefix_len, live_rows, norm_gain, w_query, w_keyval, w_out
    )
    outgoing = jnp.where(
        present[:, None, None], local_rows[chosen], jnp.zeros((), local_rows.dtype)
    )
    arrived, labels_arrived = (
        lax.all_to_all(outgoing, "dp", split_axis=0, concat_axis=0, tiled=True),
        lax.all_to_all(labels, "dp", split_axis=0, concat_axis=0, tiled=True),
    )
    source = jnp.argmax(labels_arrived[None, :] == slot_ids[:, None], axis=1)
    result = arrived[source]
    return (result, new_kv)


LINE = 4
CHUNK = 128
GROUPS = (8, 4, 1)


def pick_of(info_ref, turn, holding):
    target = info_ref[1] ^ turn
    pick = 0
    for place in range(1, holding):
        pick = jnp.where(info_ref[2 + place] == target, place, pick)
    return pick


def norm_kernel(info_ref, hidden_ref, gain_ref, *out_refs):
    step = pl.program_id(0)
    widened = hidden_ref[0].astype(jnp.float32)
    mean = jnp.mean(widened * widened, axis=-1, keepdims=True)
    gain = gain_ref[...].astype(jnp.float32)[None, :]
    normed = (widened * lax.rsqrt(mean + EPSILON) * gain).astype(jnp.bfloat16)
    for place, out_ref in enumerate(out_refs):
        @pl.when(step == place)
        def _():
            out_ref[...] = normed


def norm_some(info, turns, hidden, gain):
    holding, rows, width = hidden.shape

    def chosen(i, info_ref):
        turn = jnp.int32(turns[0])
        for place in range(1, len(turns)):
            turn = jnp.where(i == place, turns[place], turn)
        return (pick_of(info_ref, turn, holding), 0, 0)

    return pl.pallas_call(
        norm_kernel,
        grid_spec=pltpu.PrefetchScalarGridSpec(
            num_scalar_prefetch=1,
            grid=(len(turns),),
            in_specs=[
                pl.BlockSpec((1, rows, width), chosen),
                pl.BlockSpec((width,), lambda i, info_ref: (0,)),
            ],
            out_specs=[pl.BlockSpec((rows, width), lambda i, info_ref: (0, 0))] * len(turns),
        ),
        out_shape=[jax.ShapeDtypeStruct((rows, width), jnp.bfloat16)] * len(turns),
        compiler_params=pltpu.CompilerParams(vmem_limit_bytes=GRANT),
        cost_estimate=pl.CostEstimate(
            flops=4 * rows * width * len(turns),
            bytes_accessed=4 * rows * width * len(turns),
            transcendentals=rows,
        ),
        name="norm_some",
    )(info, *stored_of(hidden), gain)


def load_kernel(count, *refs):
    sources, kept, sems = refs[:count], refs[-1 - count : -1], refs[-1]
    copies = [
        pltpu.make_async_copy(sources[place], kept[place], sems.at[place]) for place in range(count)
    ]
    for item in copies:
        item.start()
    for item in copies:
        item.wait()


def load(*arrays, after=()):
    kept = pl.BlockSpec(memory_space=pltpu.MemorySpace.VMEM)
    return pl.pallas_call(
        functools.partial(load_kernel, len(arrays)),
        in_specs=[HBM] * (len(arrays) + len(after)),
        out_specs=[kept] * len(arrays),
        out_shape=[pltpu.VMEM(item.shape, item.dtype) for item in arrays],
        scratch_shapes=[pltpu.SemaphoreType.DMA((len(arrays),))],
        compiler_params=pltpu.CompilerParams(vmem_limit_bytes=GRANT),
        name="load",
    )(*stored_of(*arrays), *after)


def stored_of(*arrays):
    return [pltpu.with_memory_space_constraint(item, pltpu.MemorySpace.HBM) for item in arrays]


def resident_of(*arrays):
    return [pltpu.with_memory_space_constraint(item, pltpu.MemorySpace.VMEM) for item in arrays]


def project_kernel(count, share, places, turn, holding, head_width, tile, aliased, info_ref, *refs):
    sources = refs[:count]
    query_ref, pair_ref, cosine_ref, sine_ref = refs[count : count + 4]
    refs = refs[count + 4 + aliased :]
    turned_ref, kept_ref, placed_ref = refs[:3]
    rows_ref, sems = refs[3:]
    wide = query_ref.shape[1]
    rank = info_ref[0]
    live = info_ref[2 + 2 * holding + pick_of(info_ref, turn, holding)]

    def copy(place):
        source, half = places[place][:2]
        start = pl.multiple_of(places[place][2](rank), share)
        return pltpu.make_async_copy(
            sources[source].at[pl.ds(half * share, share)],
            rows_ref.at[pl.ds(start, share)],
            sems.at[place],
        )

    for place in range(len(places)):
        @pl.when(places[place][3](rank))
        def _():
            copy(place).start()
    for place in range(len(places)):
        @pl.when(places[place][3](rank))
        def _():
            copy(place).wait()

    length = rows_ref.shape[0]
    cosine = cosine_ref[0]
    sine = sine_ref[0]
    half = head_width // 2

    def turn_rows(values):
        return values * cosine + pltpu.roll(values, half, 1) * sine

    @pl.loop(0, wide // tile)
    def _(step):
        span = pl.ds(pl.multiple_of(step * tile, tile), tile)
        part = jnp.dot(rows_ref[...], query_ref[:, span], preferred_element_type=jnp.float32)
        for head in range(tile // head_width):
            turned = turn_rows(part[:, head * head_width : (head + 1) * head_width])
            place = pl.ds(pl.multiple_of((step * (tile // head_width) + head) * length, length), length)
            turned_ref[:, place] = turned.T.astype(turned_ref.dtype)

    pairs = jnp.dot(rows_ref[...], pair_ref[...], preferred_element_type=jnp.float32)
    pairs = pairs.astype(jnp.bfloat16).astype(jnp.float32)
    keys, values = pairs[:, :head_width], pairs[:, head_width:]
    row = lax.broadcasted_iota(jnp.int32, keys.shape, 0)
    keys = jnp.where(row < live, turn_rows(keys), 0.0).astype(kept_ref.dtype)
    values = jnp.where(row < live, values, 0.0).astype(kept_ref.dtype)
    for target in (kept_ref, placed_ref.at[0]):
        target[:, :head_width] = keys
        target[:, head_width:] = values


def project(info, turn, sources, places, w_query, w_keyval, cosine, sine, placed):
    share = sources[0].shape[0]
    width, wide = w_query.shape
    narrow = w_keyval.shape[1]
    holding, length, head_width = cosine.shape
    tile = min(wide, 2 * head_width)
    resident = pl.BlockSpec(memory_space=pltpu.MemorySpace.VMEM)
    picked = lambda i, info_ref: (pick_of(info_ref, turn, holding), 0, 0)
    fixed = lambda i, info_ref: (0, 0)
    lanes = wide // head_width * length
    extra = [] if placed is None else [placed]
    return pl.pallas_call(
        functools.partial(
            project_kernel, len(sources), share, places, turn, holding, head_width, tile, len(extra)
        ),
        grid_spec=pltpu.PrefetchScalarGridSpec(
            num_scalar_prefetch=1,
            grid=(1,),
            in_specs=[HBM] * len(sources)
            + [resident] * 2
            + [pl.BlockSpec((1, length, head_width), picked)] * 2
            + [HBM] * len(extra),
            out_specs=[
                pl.BlockSpec((head_width, lanes), fixed),
                pl.BlockSpec((length, narrow), fixed),
                pl.BlockSpec((1, length, narrow), picked),
            ],
            scratch_shapes=[
                pltpu.VMEM((length, width), jnp.bfloat16),
                pltpu.SemaphoreType.DMA((len(places),)),
            ],
        ),
        out_shape=[
            jax.ShapeDtypeStruct((head_width, lanes), jnp.bfloat16),
            jax.ShapeDtypeStruct((length, narrow), jnp.bfloat16),
            jax.ShapeDtypeStruct((holding, length, narrow), jnp.bfloat16),
        ],
        input_output_aliases={len(sources) + 5: 2} if extra else {},
        compiler_params=pltpu.CompilerParams(vmem_limit_bytes=GRANT),
        cost_estimate=pl.CostEstimate(
            flops=2 * length * width * (wide + narrow),
            bytes_accessed=2 * length * width,
            transcendentals=0,
        ),
        name="project",
    )(info, *stored_of(*sources), *resident_of(w_query, w_keyval), cosine, sine, *extra)


def stretch_kernel(
    count, part, pieces, turn, holding, limit, length, tile, info_ref, turned_ref, kept_ref, cache_ref, out_w_ref, *refs
):
    outs = refs[:count]
    stored, product, heads_ref, top_ref, sum_ref, acc_ref, page_sems, out_sems = refs[count:]
    block = cache_ref.shape[1]
    head_width = kept_ref.shape[1] // 2
    lanes = turned_ref.shape[1]
    rank = info_ref[0]
    pick = pick_of(info_ref, turn, holding)
    pages = info_ref[2 + holding + pick] // block
    live = info_ref[2 + 2 * holding + pick]
    base = 2 + 3 * holding + pick * limit
    tiles = product.shape[0]
    scale = (1.0 / math.sqrt(head_width)) * math.log2(math.e)

    def page_copy(place):
        start = pl.multiple_of(place * block, block)
        return pltpu.make_async_copy(
            cache_ref.at[info_ref[base + place]], stored.at[pl.ds(start, block)], page_sems.at[place]
        )

    @pl.loop(0, pages)
    def _(place):
        page_copy(place).start()

    def fold(keys, values, mask):
        def score(first):
            return jnp.dot(keys, turned_ref[:, first : first + chunk], preferred_element_type=jnp.float32)

        firsts = list(range(0, lanes, chunk))
        coming = score(0)
        flipped = values.T
        waiting = None

        def settle(first, exps, summed, fade):
            span = slice(first, first + chunk)
            taken = jnp.dot(flipped, exps, preferred_element_type=jnp.float32)
            if mask is not None:
                sum_ref[:, span] = summed
                acc_ref[:, span] = taken
            else:
                sum_ref[:, span] = sum_ref[:, span] * fade + summed
                acc_ref[:, span] = acc_ref[:, span] * fade + taken

        for place, first in enumerate(firsts):
            span = slice(first, first + chunk)
            scores = coming
            if place + 1 < len(firsts):
                coming = score(firsts[place + 1])
            if mask is not None:
                scores = jnp.where(mask, scores, MASKED)
                top = jnp.max(scores, axis=0, keepdims=True)
                fade = None
            else:
                old = top_ref[:, span]
                top = jnp.maximum(old, jnp.max(scores, axis=0, keepdims=True))
                fade = jnp.exp2((old - top) * scale)
            exps = jnp.exp2((scores - top) * scale)
            top_ref[:, span] = top
            if waiting is not None:
                settle(*waiting)
            waiting = (first, exps.astype(jnp.bfloat16), jnp.sum(exps, axis=0, keepdims=True), fade)
        settle(*waiting)

    chunk = min(lanes, CHUNK)
    key_row = lax.broadcasted_iota(jnp.int32, (length, chunk), 0)
    query_row = lax.rem(lax.broadcasted_iota(jnp.int32, (length, chunk), 1), length)
    fold(kept_ref[:, :head_width], kept_ref[:, head_width:], (key_row <= query_row) & (key_row < live))

    def fold_span(first, span):
        for item in range(span):
            page_copy(first + item).wait()
        rows = pl.ds(pl.multiple_of(first * block, block), span * block)
        fold(stored[rows, :head_width], stored[rows, head_width:], None)

    done = 0
    for span in GROUPS:
        span = min(span, limit)
        until = pages // span

        @pl.loop(done // span, until)
        def _(step):
            fold_span(step * span, span)

        done = until * span

    share = acc_ref[...] / sum_ref[...]
    row = lax.broadcasted_iota(jnp.int32, (length, head_width), 0)
    for head in range(lanes // length):
        span = slice(head * length, (head + 1) * length)
        heads_ref[:, head * head_width : (head + 1) * head_width] = jnp.where(
            row < live, share[:, span].T, 0.0
        ).astype(heads_ref.dtype)

    def out_copies(place):
        copies = []
        for item, (out, half, row_start) in enumerate(pieces):
            start = pl.multiple_of(row_start(rank), part)
            columns = pl.ds(pl.multiple_of(place * tile, tile), tile)
            copies.append(
                pltpu.make_async_copy(
                    product.at[place, pl.ds(start, part)],
                    outs[out].at[pl.ds(half * part, part), columns],
                    out_sems.at[item, place],
                )
            )
        return copies

    @pl.loop(0, tiles)
    def _(place):
        columns = pl.ds(pl.multiple_of(place * tile, tile), tile)
        product[place] = jnp.dot(
            heads_ref[...], out_w_ref[:, columns], preferred_element_type=jnp.float32
        ).astype(product.dtype)
        for item in out_copies(place):
            item.start()

    @pl.loop(0, tiles)
    def _(place):
        for item in out_copies(place):
            item.wait()


def attend_stretch(info, turn, turned, kept, cache, w_out, sizes, pieces, part, holding, limit, length):
    head_width, lanes = turned.shape
    block = cache.shape[1]
    inner, width = w_out.shape
    tile = min(width, 1024)
    tiles = width // tile
    return pl.pallas_call(
        functools.partial(
            stretch_kernel, len(sizes), part, pieces, turn, holding, limit, length, tile
        ),
        grid_spec=pltpu.PrefetchScalarGridSpec(
            num_scalar_prefetch=1,
            grid=(1,),
            in_specs=[
                pl.BlockSpec(turned.shape, lambda i, info_ref: (0, 0)),
                pl.BlockSpec(kept.shape, lambda i, info_ref: (0, 0)),
                HBM,
                pl.BlockSpec(memory_space=pltpu.MemorySpace.VMEM),
            ],
            out_specs=[HBM] * len(sizes),
            scratch_shapes=[
                pltpu.VMEM((limit * block, 2 * head_width), jnp.bfloat16),
                pltpu.VMEM((tiles, length, tile), jnp.bfloat16),
                pltpu.VMEM((length, inner), jnp.bfloat16),
                pltpu.VMEM((1, lanes), jnp.float32),
                pltpu.VMEM((1, lanes), jnp.float32),
                pltpu.VMEM((head_width, lanes), jnp.float32),
                pltpu.SemaphoreType.DMA((limit,)),
                pltpu.SemaphoreType.DMA((len(pieces), tiles)),
            ],
        ),
        out_shape=[jax.ShapeDtypeStruct((size, width), jnp.bfloat16) for size in sizes],
        compiler_params=pltpu.CompilerParams(vmem_limit_bytes=GRANT),
        cost_estimate=pl.CostEstimate(
            flops=4 * lanes * head_width * limit * block + 2 * length * inner * width,
            bytes_accessed=4 * limit * block * head_width,
            transcendentals=lanes * limit * block,
        ),
        name="attend",
    )(info, turned, kept, *stored_of(cache), *resident_of(w_out))


def finish_kernel(turns, info_ref, labels_ref, *refs):
    count = len(turns) - 1
    moved_refs, terms = refs[:count], refs[count:-4]
    out_ref, last_ref, sems, last_sem = refs[-4:]
    group = info_ref[1]

    def copy(place):
        return pltpu.make_async_copy(
            moved_refs[place], out_ref.at[labels_ref[group ^ turns[place]]], sems.at[place]
        )

    for place in range(count):
        copy(place).start()
    total = terms[0][...].astype(jnp.float32)
    for term in terms[1:]:
        total += term[...].astype(jnp.float32)
    last_ref[...] = total.astype(last_ref.dtype)
    last = pltpu.make_async_copy(last_ref, out_ref.at[labels_ref[group ^ turns[count]]], last_sem)
    last.start()
    for place in range(count):
        copy(place).wait()
    last.wait()


def finish(info, labels, turns, arrived, terms):
    rows, width = terms[0].shape
    whole = pl.BlockSpec((rows, width), lambda i, *_: (0, 0))
    return pl.pallas_call(
        functools.partial(finish_kernel, turns),
        grid_spec=pltpu.PrefetchScalarGridSpec(
            num_scalar_prefetch=2,
            grid=(1,),
            in_specs=[whole] * (len(arrived) + len(terms)),
            out_specs=HBM,
            scratch_shapes=[
                pltpu.VMEM((rows, width), jnp.bfloat16),
                pltpu.SemaphoreType.DMA((len(arrived),)),
                pltpu.SemaphoreType.DMA,
            ],
        ),
        out_shape=jax.ShapeDtypeStruct((len(turns), rows, width), jnp.bfloat16),
        compiler_params=pltpu.CompilerParams(vmem_limit_bytes=GRANT),
        cost_estimate=pl.CostEstimate(
            flops=rows * width * len(terms), bytes_accessed=22 * rows * width, transcendentals=0
        ),
        name="finish",
    )(info, labels, *arrived, *terms)


def position_tables(starts, length):
    half = HEAD_DIM // 2
    frequency = ROPE_BASE ** (-jnp.arange(half, dtype=jnp.float32) / half)
    positions = starts[:, None] + jnp.arange(length, dtype=jnp.int32)[None, :]
    angles = positions.astype(jnp.float32)[..., None] * frequency
    cosine = jnp.cos(angles)
    sine = jnp.sin(angles)
    return (
        jnp.concatenate([cosine, cosine], axis=-1),
        jnp.concatenate([-sine, sine], axis=-1),
    )


def added(*terms):
    total = functools.reduce(lambda a, b: a + b, [term.astype(jnp.float32) for term in terms])
    return total.astype(jnp.bfloat16)


def paired(
    hidden, norm_gain, w_query, w_keyval, w_out, kv_cache, page_table, prefix_len, live_rows, plan
):
    groups = lax.axis_size("dp")
    group = lax.axis_index("dp")
    rank = lax.axis_index("tp")
    holding, share, _ = hidden.shape
    length = share * lax.axis_size("tp")
    limit = page_table.shape[1]
    cache = kv_cache.reshape(kv_cache.shape[0], -1, kv_cache.shape[-1])
    slot_ids = jnp.arange(holding, dtype=jnp.int32)
    info = jnp.concatenate(
        [jnp.stack([rank, group]), plan, prefix_len, live_rows, page_table.reshape(-1)]
    ).astype(jnp.int32)
    turns = list(range(groups))[::-1]
    steps = len(turns)
    sides = [(0, 1), (1, 0), (2, 3), (3, 2)]
    middle = [(1, 2), (2, 1)]
    outward = [(1, 0), (2, 3)]
    inward = [(0, 1), (3, 2)]
    is_inner = lambda r: (r == 1) | (r == 2)
    is_outer = lambda r: (r == 0) | (r == 3)
    always = lambda r: r >= 0
    block = lambda distance: lambda r: (r ^ distance) * share
    nearer = lambda r: jnp.where(is_inner(r), r ^ 3, r ^ 2) * share
    farther = lambda r: jnp.where(is_inner(r), r ^ 2, r ^ 3) * share

    (first,) = norm_some(info, turns[:1], hidden, norm_gain)
    normed = [first, *norm_some(info, turns[1:], hidden, norm_gain)]
    matches = plan[None, :] == jnp.arange(groups, dtype=jnp.int32)[:, None]
    chosen = jnp.sum(jnp.where(matches, slot_ids[None, :], 0), axis=1)
    labels = lax.all_to_all(chosen, "dp", split_axis=0, concat_axis=0, tiled=True)
    cosine, sine = position_tables(prefix_len, length)
    w_query, w_keyval = load(w_query, w_keyval, after=(labels,))
    (w_out,) = load(w_out)

    sources = []
    for step in range(steps):
        own = normed[step]
        sibling = lax.ppermute(own, "tp", sides)
        if step == 0:
            first_in = lax.ppermute(own, "tp", middle)
            second_in = lax.ppermute(sibling, "tp", middle)
            first_out = lax.ppermute(first_in, "tp", outward)
            second_out = lax.ppermute(second_in, "tp", outward)
            sources.append(
                (
                    [own, sibling, first_in, second_in, first_out, second_out],
                    [
                        (0, 0, block(0), always),
                        (1, 0, block(1), always),
                        (2, 0, block(3), is_inner),
                        (3, 0, block(2), is_inner),
                        (4, 0, block(2), is_outer),
                        (5, 0, block(3), is_outer),
                    ],
                )
            )
        else:
            pair = jnp.concatenate([own, sibling], axis=0)
            crossed = lax.ppermute(pair, "tp", middle)
            passed = lax.ppermute(crossed, "tp", outward)
            sources.append(
                (
                    [own, sibling, crossed, passed],
                    [
                        (0, 0, block(0), always),
                        (1, 0, block(1), always),
                        (2, 0, block(3), is_inner),
                        (2, 1, block(2), is_inner),
                        (3, 0, block(2), is_outer),
                        (3, 1, block(3), is_outer),
                    ],
                )
            )

    placed = None
    arrived = []
    for step, turn in enumerate(turns):
        values, places = sources[step]
        turned, kept, placed = project(
            info, turn, values, places, w_query, w_keyval, cosine, sine, placed
        )
        if step == steps - 1:
            sizes, pieces = (share,) * 4, [(d, 0, block(d)) for d in range(4)]
        else:
            sizes = (2 * share, share, share)
            pieces = [(0, 0, nearer), (0, 1, farther), (1, 0, block(1)), (2, 0, block(0))]
        parts = attend_stretch(
            info, turn, turned, kept, cache, w_out, sizes, pieces, share, holding, limit, length
        )
        if step == steps - 1:
            own, beside, beyond, across = parts
            one = lax.ppermute(across, "tp", inward)
            two = lax.ppermute(beyond, "tp", inward)
            three = lax.ppermute(beside, "tp", inward)
            four = lax.ppermute(added(beyond, one), "tp", middle)
            five = lax.ppermute(added(across, two), "tp", middle)
            six = lax.ppermute(added(beside, four), "tp", outward)
            result = finish(info, labels, turns, arrived, [own, three, five, six])
        else:
            far_part, beside, own = parts
            joined = lax.ppermute(far_part, "tp", inward)
            crossed = lax.ppermute(added(far_part, joined), "tp", middle)
            from_outer = lax.ppermute(beside, "tp", inward)
            outgoing = added(beside, crossed[share:])
            from_inner = lax.ppermute(outgoing, "tp", outward)
            branch = added(own, crossed[:share], from_outer, from_inner)
            pairs = [(g, g ^ turn) for g in range(groups)]
            arrived.append(lax.ppermute(branch, "dp", pairs))
    return (result, placed)


def per_device(
    hidden, norm_gain, w_query, w_keyval, w_out, kv_cache, page_table, prefix_len, live_rows, plan
):
    groups = lax.axis_size("dp")
    even = groups == hidden.shape[0] == LINE
    route = paired if even and lax.axis_size("tp") == KV_HEADS == LINE else general
    return route(
        hidden, norm_gain, w_query, w_keyval, w_out, kv_cache, page_table, prefix_len, live_rows, plan
    )


def solution(mesh):
    in_specs = (
        P(("parts", "dp"), "tp", None),
        P(),
        P(None, "tp"),
        P(None, "tp"),
        P("tp", None),
        P(("parts", "dp"), "tp", None, None),
        P(("parts", "dp"), None),
        P(("parts", "dp")),
        P(("parts", "dp")),
        P(("parts", "dp")),
    )
    out_specs = (P(("parts", "dp"), "tp", None), P(("parts", "dp"), None, "tp"))
    return jax.shard_map(
        per_device, mesh=mesh, in_specs=in_specs, out_specs=out_specs, check_vma=False
    )
```
